512 devices in a mesh: facet: 16 (over z), sub: 8 (over x, core), vis: 4 (over y).
Axes of the slice: x: 4, y: 4, z: 16, core: 2. Of those that a mesh axis runs over, the one named last changes fastest.
Arguments:
- sky: float32 [8192, 512], P(('facet', 'vis')), may hold values from -6 to 6
- row_offsets: int32 [8], P('sub'), may hold values from 0 to 7936
- block_counts: int32 [512], P(('facet', 'sub', 'vis')), may hold values from 1 to 16, as said below
- block_ids: int32 [8192], P(('facet', 'sub', 'vis')), may hold values from 0 to 127
- kernel_rows: float32 [8192, 8, 128], P(('facet', 'sub', 'vis')), may hold values from -2 to 2
- kernel_cols: float32 [8192, 128, 128], P(('facet', 'sub', 'vis')), may hold values from -0.5 to 0.5
- observed: float32 [8192, 2, 128], P(('facet', 'sub', 'vis')), may hold values from -6 to 6
- weights: int32 [8192, 128], P(('facet', 'sub', 'vis')), may hold values from 1 to 4
Outputs:
- residual_image: float32 [8192, 512], P(('facet', 'vis'))
- residual_vis: float32 [8192, 2, 128], P(('facet', 'sub', 'vis'))
The draws below stay inside these ranges and needn't reach their ends.
Inputs may be any that keep to these rules, and one draw needn't show every extreme that they name: `block_counts`: every device has at most 16 live slots, the first ones; some device has exactly 16.
All inputs are finite; a program needn't handle non-finite values.
Results may differ from the reference program's by a relative error of at most 0.0003.
Values sent between devices are 32-bit elements; how exact they have to be, the bound alone decides.
No kernel may reach another device: no remote copies, remote signals or barrier semaphores. Data moves between devices by JAX's collectives and lax.ppermute only.
A program may use at most 64 MiB of HBM per device.

```python
import jax
import jax.numpy as jnp
from jax import lax

K = 512
CR = 256
BR = 8
BC = 128
VB = 128
NB = 16
NBLK = 128
NK = 8192
SUBGRIDS = 8
VBLOCKS = 8192
N_FACET = 16
N_SUB = 8
N_VIS = 4
DEVICES = 512


def draw_block_counts(key, part):
    flat = jnp.arange(DEVICES, dtype=jnp.int32)
    column = flat // N_VIS % N_SUB
    upper = jnp.maximum(1, NB * (column + 1) // N_SUB)
    raw = jax.random.randint(key, (DEVICES,), 0, 1048576, dtype=jnp.int32)
    counts = 1 + raw % upper
    return jnp.where(flat == 0, NB, counts).astype(jnp.int32)


def plant(entries, own_key, smallest, top_value):
    dims = entries.shape
    index_at = [jax.random.randint(jax.random.fold_in(own_key, axis), (), 0, dims[axis]) for axis in range(len(dims))]
    entries = entries.at[tuple(index_at)].set(smallest)
    longest = dims.index(max(dims))
    index_at[longest] = (index_at[longest] + 1) % dims[longest]
    return entries.at[tuple(index_at)].set(top_value)


def levels(stream_key, dims, cuts, low, high):
    level = 1.0
    for axis_at, parts in cuts:
        draws = jax.random.uniform(jax.random.fold_in(jax.random.fold_in(stream_key, 6), axis_at), (parts,), jnp.float32, low / len(cuts), high / len(cuts))
        level = level * jnp.repeat(jnp.exp(draws), dims[axis_at] // parts).reshape((-1,) + (1,) * (len(dims) - 1 - axis_at))
    return level


def centred(key, dims, width, reach, shards=(), kind=jnp.bfloat16):
    array = jax.random.normal(key, dims, jnp.float32) * width
    if len(shards) > 0:
        array = levels(key, dims, shards, -0.22, 0.18) * array
    return jnp.clip(array, min=-reach, max=reach).astype(kind)


def setup_inputs(seed: int = 0) -> dict:
    streams_of = jax.random.split(jax.random.key(seed), 9)
    sky = centred(streams_of[0], (NK, K), 1.0, 6.0, ((0, 64),), jnp.float32)
    row_offsets = plant(jax.random.randint(streams_of[1], (SUBGRIDS,), 0, NK - CR + 1), jax.random.fold_in(streams_of[1], 1), 0, NK - CR).astype(jnp.int32)
    block_counts = draw_block_counts(jax.random.fold_in(streams_of[8], 71), 0)
    block_ids = plant(jax.random.randint(streams_of[3], (VBLOCKS,), 0, NBLK), jax.random.fold_in(streams_of[3], 1), 0, NBLK - 1).astype(jnp.int32)
    kernel_rows = centred(streams_of[4], (VBLOCKS, BR, VB), BR ** -0.5, 2.0, ((0, 512),), jnp.float32)
    kernel_cols = centred(streams_of[5], (VBLOCKS, BC, VB), BC ** -0.5, 0.5, ((0, 512),), jnp.float32)
    observed = centred(streams_of[6], (VBLOCKS, 2, VB), 1.0, 6.0, ((0, 512),), jnp.float32)
    weights = plant(jax.random.randint(streams_of[7], (VBLOCKS, VB), 1, 5), jax.random.fold_in(streams_of[7], 1), 1, 4).astype(jnp.int32)
    return {"sky": sky, "row_offsets": row_offsets, "block_counts": block_counts, "block_ids": block_ids, "kernel_rows": kernel_rows, "kernel_cols": kernel_cols, "observed": observed, "weights": weights}


def highest_dot(left, right):
    return jnp.dot(left, right, precision=lax.Precision.HIGHEST, preferred_element_type=jnp.float32)


def column_tables():
    index_k = jnp.arange(K, dtype=jnp.int32)
    product = (index_k[:, None] * index_k[None, :]) % K
    angle = product.astype(jnp.float32) * (2.0 * jnp.pi / K)
    scale = K ** -0.5
    return jnp.cos(angle) * scale, jnp.sin(angle) * scale


def row_tables(starts, pixels, total):
    product = (starts[:, None] * pixels[None, :]) % total
    angle = product.astype(jnp.float32) * (2.0 * jnp.pi / total)
    scale = total ** -0.5
    return jnp.cos(angle) * scale, jnp.sin(angle) * scale


def column_forward(real_part, imag_part, cos_cols, sin_cols):
    grid_real = highest_dot(real_part, cos_cols) + highest_dot(imag_part, sin_cols)
    grid_imag = highest_dot(imag_part, cos_cols) - highest_dot(real_part, sin_cols)
    return jnp.stack([grid_real, grid_imag], axis=1)


def column_adjoint(subgrid, cos_cols, sin_cols):
    grid_real = subgrid[:, 0]
    grid_imag = subgrid[:, 1]
    back_real = highest_dot(grid_real, cos_cols) - highest_dot(grid_imag, sin_cols)
    back_imag = highest_dot(grid_imag, cos_cols) + highest_dot(grid_real, sin_cols)
    return jnp.stack([back_real, back_imag], axis=1)


def degrid_grid(subgrid, live_count, block_index, kernel_rows, kernel_cols, observed, weights):
    band_rows = CR // BR
    band_cols = K // BC
    nblocks = band_rows * band_cols
    block_table = subgrid.reshape(band_rows, BR, 2, band_cols, BC).transpose(0, 3, 1, 2, 4).reshape(nblocks, BR, 2, BC)
    onehot = (block_index[:, None] == jnp.arange(nblocks, dtype=jnp.int32)[None, :]).astype(jnp.float32)
    hp = lax.Precision.HIGHEST
    chosen = jnp.einsum('bn,nrzc->brzc', onehot, block_table, precision=hp)
    along = jnp.einsum('brzc,bct->brzt', chosen, kernel_cols, precision=hp)
    model = jnp.sum(along * kernel_rows[:, :, None, :], axis=1)
    live = (jnp.arange(observed.shape[0], dtype=jnp.int32) < live_count)[:, None, None]
    residual = jnp.where(live, weights[:, None, :].astype(jnp.float32) * (observed - model), jnp.zeros_like(model))
    spread = kernel_rows[:, :, None, :] * residual[:, None, :, :]
    back = jnp.einsum('brzt,bct->brzc', spread, kernel_cols, precision=hp)
    table_back = jnp.einsum('bn,brzc->nrzc', onehot, back, precision=hp)
    partial_value = table_back.reshape(band_rows, band_cols, BR, 2, BC).transpose(0, 2, 3, 1, 4).reshape(CR, 2, K)
    return residual, partial_value


def reference(sky, row_offsets, block_counts, block_ids, kernel_rows, kernel_cols, observed, weights):
    total = N_FACET * K
    cos_cols, sin_cols = column_tables()
    pixel_all = jnp.arange(total, dtype=jnp.int32)

    def forward(offset):
        starts = offset + jnp.arange(CR, dtype=jnp.int32)
        cos_rows, sin_rows = row_tables(starts, pixel_all, total)
        real_part = highest_dot(cos_rows, sky)
        imag_part = -highest_dot(sin_rows, sky)
        return column_forward(real_part, imag_part, cos_cols, sin_cols)

    grids = lax.map(forward, row_offsets)
    devices = N_FACET * N_SUB * N_VIS

    def per_device(summed, inputs):
        index, count, ids, rows_k, cols_k, seen, wts = inputs
        column = (index // N_VIS) % N_SUB
        residual, partial_value = degrid_grid(grids[column], count, ids, rows_k, cols_k, seen, wts)
        summed = summed.at[column].add(partial_value)
        return summed, residual

    initial_sum = jnp.zeros((N_SUB, CR, 2, K), jnp.float32)
    summed, residual = lax.scan(per_device, initial_sum, (
        jnp.arange(devices, dtype=jnp.int32), block_counts, block_ids.reshape(devices, NB),
        kernel_rows.reshape(devices, NB, BR, VB), kernel_cols.reshape(devices, NB, BC, VB),
        observed.reshape(devices, NB, 2, VB), weights.reshape(devices, NB, VB)))

    def accumulate(running, pair):
        offset, residual_grid = pair
        adjoint = column_adjoint(residual_grid, cos_cols, sin_cols)
        starts = offset + jnp.arange(CR, dtype=jnp.int32)
        cos_rows, sin_rows = row_tables(starts, pixel_all, total)
        running = running + highest_dot(cos_rows.T, adjoint[:, 0]) - highest_dot(sin_rows.T, adjoint[:, 1])
        return running, None

    image, unused = lax.scan(accumulate, jnp.zeros((total, K), jnp.float32), (row_offsets, summed))
    return image, residual.reshape(devices * NB, 2, VB)
```

```python
import jax
import jax.numpy as jnp
import numpy as np
from jax import lax
from jax.sharding import PartitionSpec as P

K = 512
CR = 256
BR = 8
BC = 128
SUBS = 8
RANK = 32
RANKS = 16
HIGH = lax.Precision.HIGH


def prolate(count, band, total, rank):
    j = np.arange(count, dtype=np.float64)
    diag = -np.cos(np.pi * (2 * j - count + 1) / total) * np.cos(np.pi * band / total)
    m = np.arange(1, count, dtype=np.float64)
    off = np.sin(np.pi * m / total) * np.sin(np.pi * (count - m) / total)
    values, vectors = np.linalg.eigh(np.diag(diag) + np.diag(off, 1) + np.diag(off, -1))
    basis = vectors[:, ::-1][:, :rank]
    signs = np.sign(np.sum(basis[count // 2 :], axis=0))
    return basis * signs


def constants(facets, vises, total):
    rows = K // vises
    lanes = K // vises
    bands = K // BC
    sub_lanes = BC // vises
    basis = prolate(K, CR, total, RANK)
    section = prolate(rows, CR, total, RANKS)
    merge = np.stack([section.T @ basis[v * rows : (v + 1) * rows] for v in range(vises)])
    r = np.arange(CR) - (CR - 1) / 2
    p = np.arange(K) - (K - 1) / 2
    kernel = np.exp(-2j * np.pi * np.outer(r, p) / total) @ basis
    centres = np.arange(facets) * K + (K - 1) / 2
    shift = np.exp(-2j * np.pi * np.outer(r, centres) / total)
    expand = shift[:, :, None] * kernel[:, None, :] * total**-0.5
    real, imag = expand.real, expand.imag
    spread = np.stack(
        [np.stack([real, -imag], axis=2), np.stack([imag, real], axis=2)], axis=0
    )
    spread = spread.reshape(2, CR // BR, BR, facets * 2 * RANK).transpose(1, 0, 2, 3)
    spread = spread.reshape(2 * CR, facets * 2 * RANK)
    merges = np.zeros((2, RANK, vises, 2, RANKS))
    for part in range(2):
        merges[part, :, :, part, :] = merge.transpose(2, 0, 1)
    merges = merges.reshape(2 * RANK, vises * 2 * RANKS)
    column = np.arange(K).reshape(bands, vises, sub_lanes).transpose(1, 0, 2).reshape(vises, lanes)
    angle = 2 * np.pi * ((np.arange(K)[None, :, None] * column[:, None, :]) % K) / K
    table = np.concatenate([np.cos(angle), np.sin(angle)], axis=2) * K**-0.5
    return tuple(np.asarray(x, np.float32) for x in (section.T, merges, spread, table))


def dot(spec, left, right):
    return jnp.einsum(spec, left, right, precision=HIGH, preferred_element_type=jnp.float32)


def shards(sky, row_offsets, block_counts, block_ids, kernel_rows, kernel_cols, observed, weights):
    facets = lax.axis_size("facet")
    vises = lax.axis_size("vis")
    subs = lax.axis_size("sub")
    total = facets * K
    rows = sky.shape[0]
    lanes = K // vises
    slots = block_ids.shape[0]
    bands = K // BC
    row_bands = CR // BR
    groups = slots // vises
    sub_lanes = BC // vises
    section, merges, spread, table = constants(facets, vises, total)

    first = (lax.axis_index("facet") * vises + lax.axis_index("vis")) * rows
    pixels = first + jnp.arange(rows, dtype=jnp.int32)

    def phases(offsets):
        product = ((2 * offsets + (CR - 1)) * pixels) % (2 * total)
        angle = product.astype(jnp.float32) * (2.0 * jnp.pi / (2 * total))
        return jnp.cos(angle), jnp.sin(angle)

    cos_p, sin_p = phases(row_offsets[0])
    into = jnp.concatenate([section * cos_p, -section * sin_p], axis=0)
    coef = dot("mp,pk->mk", into, sky)
    both = dot("mk,vkc->vmc", coef, table)
    real = both[:, :RANKS, :lanes] + both[:, RANKS:, lanes:]
    imag = both[:, RANKS:, :lanes] - both[:, :RANKS, lanes:]
    ids_rows = jnp.broadcast_to(
        block_ids.astype(jnp.float32)[None, :, None], (vises, slots, lanes)
    )
    sent = jnp.concatenate([real, imag, ids_rows], axis=1)
    got = lax.all_to_all(sent, "vis", 0, 0, tiled=True)
    ids = got[:, 2 * RANKS :, 0].astype(jnp.int32).reshape(vises * slots)
    facet_coef = dot("kx,xl->kl", merges, got[:, : 2 * RANKS].reshape(vises * 2 * RANKS, lanes))
    sent = jnp.broadcast_to(facet_coef[None], (facets, 2 * RANK, lanes))
    got = lax.all_to_all(sent, "facet", 0, 0, tiled=True)

    grid = dot("gx,xl->gl", spread, got.reshape(facets * 2 * RANK, lanes))
    onehot = (ids[:, None] == jnp.arange(row_bands * bands, dtype=jnp.int32)[None, :]).astype(
        jnp.float32
    )
    blocks = (
        grid.reshape(row_bands, 2 * BR, bands, sub_lanes)
        .transpose(0, 2, 1, 3)
        .reshape(row_bands * bands, 2 * BR * sub_lanes)
    )
    picked = dot("sn,nx->sx", onehot, blocks)
    sent = (
        picked.reshape(vises, groups, vises, 2 * BR, sub_lanes)
        .transpose(0, 1, 3, 2, 4)
        .reshape(vises, groups * 2 * BR, lanes)
    )
    got = lax.all_to_all(sent, "vis", 0, 0, tiled=True)
    chosen = (
        got.reshape(vises, groups, 2 * BR, vises, sub_lanes)
        .transpose(1, 3, 2, 0, 4)
        .reshape(slots, 2, BR, BC)
    )

    along = dot("szrc,sct->szrt", chosen, kernel_cols)
    model = jnp.sum(along * kernel_rows[:, None, :, :], axis=2)
    live = (jnp.arange(slots, dtype=jnp.int32) < block_counts[0])[:, None, None]
    residual = jnp.where(
        live, weights[:, None, :].astype(jnp.float32) * (observed - model), jnp.zeros_like(model)
    )
    back = dot(
        "szrt,sct->szrc", kernel_rows[:, None, :, :] * residual[:, :, None, :], kernel_cols
    )

    sent = (
        back.reshape(groups, vises, 2 * BR, vises, sub_lanes)
        .transpose(3, 0, 2, 1, 4)
        .reshape(vises, groups * 2 * BR, lanes)
    )
    got = lax.all_to_all(sent, "vis", 0, 0, tiled=True)
    parts = (
        got.reshape(vises, groups, 2 * BR, vises, sub_lanes)
        .transpose(0, 1, 3, 2, 4)
        .reshape(vises * slots, 2 * BR * sub_lanes)
    )
    summed = dot("sn,sx->nx", onehot, parts)
    residual_grid = (
        summed.reshape(row_bands, bands, 2 * BR, sub_lanes)
        .transpose(0, 2, 1, 3)
        .reshape(2 * CR, lanes)
    )
    sent = dot("gx,gl->xl", spread, residual_grid).reshape(facets, 2 * RANK, lanes)
    got = lax.all_to_all(sent, "facet", 0, 0, tiled=True)
    facet_coef = jnp.sum(got, axis=0)

    coef = dot("kx,kl->xl", merges, facet_coef).reshape(1, vises, 2 * RANKS, lanes)
    offset_rows = jnp.broadcast_to(
        row_offsets[0].astype(jnp.float32), (subs, vises, 8, lanes)
    )
    sent = jnp.concatenate(
        [jnp.broadcast_to(coef, (subs, vises, 2 * RANKS, lanes)), offset_rows], axis=2
    ).reshape(subs * vises, 2 * RANKS + 8, lanes)
    got = lax.all_to_all(sent, ("sub", "vis"), 0, 0, tiled=True)
    got = got.reshape(subs, vises, 2 * RANKS + 8, lanes)
    offsets = got[:, 0, 2 * RANKS, 0].astype(jnp.int32)
    cos_q, sin_q = phases(offsets[:, None])
    cos_q = section[None] * cos_q[:, None, :]
    sin_q = section[None] * sin_q[:, None, :]
    out = jnp.stack(
        [
            jnp.concatenate([cos_q, -sin_q], axis=1),
            jnp.concatenate([sin_q, cos_q], axis=1),
        ],
        axis=0,
    )
    pixels_cols = dot("zqap,qval->zpvl", out, got[:, :, : 2 * RANKS])
    image = dot("pvl,vkl->pk", pixels_cols[0], table[:, :, :lanes]) - dot(
        "pvl,vkl->pk", pixels_cols[1], table[:, :, lanes:]
    )
    return (image, residual)


def solution(mesh):
    return jax.shard_map(
        shards,
        mesh=mesh,
        in_specs=(
            P(("facet", "vis"), None),
            P("sub"),
            P(("facet", "sub", "vis")),
            P(("facet", "sub", "vis")),
            P(("facet", "sub", "vis"), None, None),
            P(("facet", "sub", "vis"), None, None),
            P(("facet", "sub", "vis"), None, None),
            P(("facet", "sub", "vis"), None),
        ),
        out_specs=(P(("facet", "vis"), None), P(("facet", "sub", "vis"), None, None)),
        check_vma=False,
    )
```

```python
import functools

import jax
import jax.numpy as jnp
import numpy as np
from jax import lax
from jax.experimental import pallas as pl
from jax.experimental.pallas import tpu as pltpu
from jax.sharding import PartitionSpec as P

K = 512
CR = 256
BR = 8
BC = 128
SUBS = 8
RANK = 32
RANKS = 16
HIGH = lax.Precision.HIGH


def prolate(count, band, total, rank):
    j = np.arange(count, dtype=np.float64)
    diag = -np.cos(np.pi * (2 * j - count + 1) / total) * np.cos(np.pi * band / total)
    m = np.arange(1, count, dtype=np.float64)
    off = np.sin(np.pi * m / total) * np.sin(np.pi * (count - m) / total)
    values, vectors = np.linalg.eigh(np.diag(diag) + np.diag(off, 1) + np.diag(off, -1))
    basis = vectors[:, ::-1][:, :rank]
    signs = np.sign(np.sum(basis[count // 2 :], axis=0))
    return basis * signs


def constants(facets, vises, total):
    rows = K // vises
    lanes = K // vises
    bands = K // BC
    sub_lanes = BC // vises
    basis = prolate(K, CR, total, RANK)
    section = prolate(rows, CR, total, RANKS)
    merge = np.stack([section.T @ basis[v * rows : (v + 1) * rows] for v in range(vises)])
    r = np.arange(CR) - (CR - 1) / 2
    p = np.arange(K) - (K - 1) / 2
    kernel = np.exp(-2j * np.pi * np.outer(r, p) / total) @ basis
    centres = np.arange(facets) * K + (K - 1) / 2
    shift = np.exp(-2j * np.pi * np.outer(r, centres) / total)
    expand = shift[:, :, None] * kernel[:, None, :] * total**-0.5
    real, imag = expand.real, expand.imag
    spread = np.stack(
        [np.stack([real, -imag], axis=2), np.stack([imag, real], axis=2)], axis=0
    )
    spread = spread.reshape(2, CR // BR, BR, facets * 2 * RANK).transpose(1, 0, 2, 3)
    spread = spread.reshape(2 * CR, facets * 2 * RANK)
    merges = np.zeros((2, RANK, vises, 2, RANKS))
    for part in range(2):
        merges[part, :, :, part, :] = merge.transpose(2, 0, 1)
    merges = merges.reshape(2 * RANK, vises * 2 * RANKS)
    column = np.arange(K).reshape(bands, vises, sub_lanes).transpose(1, 0, 2).reshape(vises, lanes)
    angle = 2 * np.pi * ((np.arange(K)[None, :, None] * column[:, None, :]) % K) / K
    table = np.concatenate([np.cos(angle), np.sin(angle)], axis=2) * K**-0.5
    spread_high = spread.astype(jnp.bfloat16)
    spread_low = (spread - spread_high.astype(np.float64)).astype(jnp.bfloat16)
    section, merges, table = (np.asarray(x, np.float32) for x in (section.T, merges, table))
    return section, merges, (spread_high, spread_low), table


def dot(spec, left, right):
    return jnp.einsum(spec, left, right, precision=HIGH, preferred_element_type=jnp.float32)


def halves(x):
    high = x.astype(jnp.bfloat16)
    return high, (x - high.astype(jnp.float32)).astype(jnp.bfloat16)


def mxu(left, right, contract):
    return lax.dot_general(left, right, (contract, ((), ())), preferred_element_type=jnp.float32)


def product(left, right, contract):
    (lh, ll), (rh, rl) = left, right
    return mxu(lh, rh, contract) + mxu(lh, rl, contract) + mxu(ll, rh, contract)


NN = ((1,), (0,))
NT = ((1,), (1,))
TN = ((0,), (0,))


def slot_rows(ids_ref, member, vises, groups, first):
    rows = []
    for v in range(vises):
        for g in range(groups):
            at = first + vises * g + member
            rows.append(jnp.broadcast_to(ids_ref[v, at : at + 1, :], (2 * BR, BC)))
    return jnp.concatenate(rows, axis=0).astype(jnp.int32)


def selection(ids, bands):
    inner = lax.broadcasted_iota(jnp.int32, ids.shape, 0) % (2 * BR)
    target = (ids // bands) * (2 * BR) + inner
    lane = lax.broadcasted_iota(jnp.int32, ids.shape, 1)
    pieces = [
        jnp.where(target == lane + part * BC, 1.0, 0.0).astype(jnp.bfloat16)
        for part in range(2 * CR // BC)
    ]
    return jnp.concatenate(pieces, axis=1), ids % bands


def everywhere(x, width):
    step = BC // 2
    while step >= width:
        x = x + pltpu.roll(x, step, 1)
        step //= 2
    return x


def pick_kernel(vises, groups, coef_ref, ids_ref, high_ref, low_ref, out_ref):
    width = BC // vises
    grid = product((high_ref[...], low_ref[...]), halves(coef_ref[...]), NN)
    high, low = halves(grid)
    piece = lax.broadcasted_iota(jnp.int32, (vises * groups * 2 * BR, BC), 1) // width
    total = jnp.zeros((vises * groups * 2 * BR, BC), jnp.float32)
    for member in range(vises):
        ids = slot_rows(ids_ref, member, vises, groups, 2 * RANKS)
        hot, band = selection(ids, K // BC)
        rows = mxu(hot, high, NN) + mxu(hot, low, NN)
        rows = everywhere(jnp.where(piece == band, rows, 0.0), width)
        total = jnp.where(piece == member, rows, total)
    out_ref[...] = total.reshape(out_ref.shape)


def place_kernel(vises, groups, part_ref, ids_ref, high_ref, low_ref, out_ref):
    width = BC // vises
    parts = part_ref[...].reshape(vises * groups * 2 * BR, BC)
    piece = lax.broadcasted_iota(jnp.int32, parts.shape, 1) // width
    turned = jnp.zeros((BC, 2 * CR), jnp.float32)
    for member in range(vises):
        ids = slot_rows(ids_ref, member, vises, groups, 2 * RANKS)
        hot, band = selection(ids, K // BC)
        rows = everywhere(jnp.where(piece == member, parts, 0.0), width)
        high, low = halves(jnp.where(piece == band, rows, 0.0))
        turned = turned + mxu(high, hot, TN) + mxu(low, hot, TN)
    coef = product(halves(turned), (high_ref[...], low_ref[...]), NN)
    out_ref[...] = coef.T.reshape(out_ref.shape)


def degrid_kernel(vises, groups, got_ref, rows_ref, cols_ref, seen_ref, scale_ref, res_ref, out_ref):
    width = BC // vises
    piece = lax.broadcasted_iota(jnp.int32, (2 * BR, BC), 1) // width
    for g in range(groups):
        at = pl.ds(g * 2 * BR, 2 * BR)
        held = [got_ref[v, at, :] for v in range(vises)]
        backs = []
        for member in range(vises):
            slot = vises * g + member
            block = held[member]
            for v in range(vises):
                if v != member:
                    moved = pltpu.roll(held[v], (width * (v - member)) % BC, 1)
                    block = jnp.where(piece == v, moved, block)
            cols = halves(cols_ref[slot])
            along = product(halves(block), cols, NN).reshape(2, BR, BC)
            weight_rows = rows_ref[slot]
            model = jnp.sum(along * weight_rows[None], axis=1)
            residual = scale_ref[slot : slot + 1, :] * (seen_ref[slot] - model)
            res_ref[slot] = residual
            out = (weight_rows[None] * residual[:, None, :]).reshape(2 * BR, BC)
            backs.append(product(halves(out), cols, NT))
        for v in range(vises):
            sent = backs[v]
            for member in range(vises):
                if member != v:
                    moved = pltpu.roll(backs[member], (width * (member - v)) % BC, 1)
                    sent = jnp.where(piece == member, moved, sent)
            out_ref[v, at, :] = sent


def whole():
    return pl.BlockSpec(memory_space=pltpu.VMEM)


def shards(sky, row_offsets, block_counts, block_ids, kernel_rows, kernel_cols, observed, weights):
    facets = lax.axis_size("facet")
    vises = lax.axis_size("vis")
    subs = lax.axis_size("sub")
    total = facets * K
    rows = sky.shape[0]
    lanes = K // vises
    slots = block_ids.shape[0]
    groups = slots // vises
    section, merges, spread, table = constants(facets, vises, total)

    first = (lax.axis_index("facet") * vises + lax.axis_index("vis")) * rows
    pixels = first + jnp.arange(rows, dtype=jnp.int32)

    live = jnp.arange(slots, dtype=jnp.int32)[:, None] < block_counts[0]
    scale = jnp.where(live, weights.astype(jnp.float32), 0.0)
    offset_value = row_offsets[0].astype(jnp.float32)

    def phases(offsets):
        product = ((2 * offsets + (CR - 1)) * pixels) % (2 * total)
        angle = product.astype(jnp.float32) * (2.0 * jnp.pi / (2 * total))
        return jnp.cos(angle), jnp.sin(angle)

    cos_p, sin_p = phases(row_offsets[0])
    into = jnp.concatenate([section * cos_p, -section * sin_p], axis=0)
    coef = dot("mp,pk->mk", into, sky)
    both = dot("mk,vkc->vmc", coef, table)
    real = both[:, :RANKS, :lanes] + both[:, RANKS:, lanes:]
    imag = both[:, RANKS:, :lanes] - both[:, :RANKS, lanes:]
    ids_rows = jnp.broadcast_to(
        block_ids.astype(jnp.float32)[None, :, None], (vises, slots, lanes)
    )
    sent = jnp.concatenate([real, imag, ids_rows], axis=1)
    sent, scale, offset_value, pixels = lax.optimization_barrier(
        (sent, scale, offset_value, pixels)
    )
    got = lax.all_to_all(sent, "vis", 0, 0, tiled=True)
    held = got
    facet_coef = dot("kx,xl->kl", merges, got[:, : 2 * RANKS].reshape(vises * 2 * RANKS, lanes))
    sent = jnp.broadcast_to(facet_coef[None], (facets, 2 * RANK, lanes))
    got = lax.all_to_all(sent, "facet", 0, 0, tiled=True)

    high, low = (jnp.asarray(x) for x in spread)
    sent = pl.pallas_call(
        functools.partial(pick_kernel, vises, groups),
        out_shape=jax.ShapeDtypeStruct((vises, groups * 2 * BR, lanes), jnp.float32),
        in_specs=[whole()] * 4,
        out_specs=whole(),
        compiler_params=pltpu.CompilerParams(vmem_limit_bytes=16 << 20),
        name="pick",
    )(got.reshape(facets * 2 * RANK, lanes), held, high, low)
    got = lax.all_to_all(sent, "vis", 0, 0, tiled=True)
    residual, sent = pl.pallas_call(
        functools.partial(degrid_kernel, vises, groups),
        out_shape=(
            jax.ShapeDtypeStruct((slots, 2, BC), jnp.float32),
            jax.ShapeDtypeStruct((vises, groups * 2 * BR, lanes), jnp.float32),
        ),
        in_specs=[whole()] * 5,
        out_specs=(whole(), whole()),
        compiler_params=pltpu.CompilerParams(vmem_limit_bytes=16 << 20),
        name="degrid",
    )(got, kernel_rows, kernel_cols, observed, scale)
    got = lax.all_to_all(sent, "vis", 0, 0, tiled=True)
    sent = pl.pallas_call(
        functools.partial(place_kernel, vises, groups),
        out_shape=jax.ShapeDtypeStruct((facets, 2 * RANK, lanes), jnp.float32),
        in_specs=[whole()] * 4,
        out_specs=whole(),
        compiler_params=pltpu.CompilerParams(vmem_limit_bytes=16 << 20),
        name="place",
    )(got, held, high, low)
    got = lax.all_to_all(sent, "facet", 0, 0, tiled=True)
    facet_coef = jnp.sum(got, axis=0)

    coef = dot("kx,kl->xl", merges, facet_coef).reshape(1, vises, 2 * RANKS, lanes)
    offset_rows = jnp.broadcast_to(offset_value, (subs, vises, 8, lanes))
    sent = jnp.concatenate(
        [jnp.broadcast_to(coef, (subs, vises, 2 * RANKS, lanes)), offset_rows], axis=2
    ).reshape(subs * vises, 2 * RANKS + 8, lanes)
    got = lax.all_to_all(sent, ("sub", "vis"), 0, 0, tiled=True)
    got = got.reshape(subs, vises, 2 * RANKS + 8, lanes)
    offsets = got[:, 0, 2 * RANKS, 0].astype(jnp.int32)
    cos_q, sin_q = phases(offsets[:, None])
    cos_q = section[None] * cos_q[:, None, :]
    sin_q = section[None] * sin_q[:, None, :]
    out = jnp.stack(
        [
            jnp.concatenate([cos_q, -sin_q], axis=1),
            jnp.concatenate([-sin_q, -cos_q], axis=1),
        ],
        axis=0,
    )
    pixels_cols = dot("zqap,qval->zpvl", out, got[:, :, : 2 * RANKS])
    pixels_cols = jnp.concatenate([pixels_cols[0], pixels_cols[1]], axis=2)
    image = dot("pvl,vkl->pk", pixels_cols, table)
    return (image, residual)


def solution(mesh):
    return jax.shard_map(
        shards,
        mesh=mesh,
        in_specs=(
            P(("facet", "vis"), None),
            P("sub"),
            P(("facet", "sub", "vis")),
            P(("facet", "sub", "vis")),
            P(("facet", "sub", "vis"), None, None),
            P(("facet", "sub", "vis"), None, None),
            P(("facet", "sub", "vis"), None, None),
            P(("facet", "sub", "vis"), None),
        ),
        out_specs=(P(("facet", "vis"), None), P(("facet", "sub", "vis"), None, None)),
        check_vma=False,
    )
```

```python
import functools

import jax
import jax.numpy as jnp
import numpy as np
from jax import lax
from jax.experimental import pallas as pl
from jax.experimental.pallas import tpu as pltpu
from jax.sharding import PartitionSpec as P

K = 512
CR = 256
BR = 8
BC = 128
SUBS = 8
RANK = 28
RANKS = 16
SPARE = RANKS - 1
HIGH = lax.Precision.HIGH


def prolate(count, band, total, rank):
    j = np.arange(count, dtype=np.float64)
    diag = -np.cos(np.pi * (2 * j - count + 1) / total) * np.cos(np.pi * band / total)
    m = np.arange(1, count, dtype=np.float64)
    off = np.sin(np.pi * m / total) * np.sin(np.pi * (count - m) / total)
    values, vectors = np.linalg.eigh(np.diag(diag) + np.diag(off, 1) + np.diag(off, -1))
    basis = vectors[:, ::-1][:, :rank]
    signs = np.sign(np.sum(basis[count // 2 :], axis=0))
    return basis * signs


def constants(facets, vises, total):
    rows = K // vises
    lanes = K // vises
    bands = K // BC
    sub_lanes = BC // vises
    basis = prolate(K, CR, total, RANK)
    section = prolate(rows, CR, total, RANKS)
    section[:, SPARE] = 0.0
    merge = np.stack([section.T @ basis[v * rows : (v + 1) * rows] for v in range(vises)])
    r = np.arange(CR) - (CR - 1) / 2
    p = np.arange(K) - (K - 1) / 2
    kernel = np.exp(-2j * np.pi * np.outer(r, p) / total) @ basis
    centres = np.arange(facets) * K + (K - 1) / 2
    shift = np.exp(-2j * np.pi * np.outer(r, centres) / total)
    expand = shift[:, :, None] * kernel[:, None, :] * total**-0.5
    real, imag = expand.real, expand.imag
    spread = np.stack(
        [np.stack([real, -imag], axis=2), np.stack([imag, real], axis=2)], axis=0
    )
    spread = spread.reshape(2, CR // BR, BR, facets * 2 * RANK).transpose(1, 0, 2, 3)
    spread = spread.reshape(2 * CR, facets * 2 * RANK)
    merges = np.zeros((2, RANK, vises, 2, RANKS))
    for part in range(2):
        merges[part, :, :, part, :] = merge.transpose(2, 0, 1)
    merges = merges.reshape(2 * RANK, vises * 2 * RANKS)
    column = np.arange(K).reshape(bands, vises, sub_lanes).transpose(1, 0, 2).reshape(vises, lanes)
    angle = 2 * np.pi * ((np.arange(K)[None, :, None] * column[:, None, :]) % K) / K
    table = np.concatenate([np.cos(angle), np.sin(angle)], axis=2) * K**-0.5
    shares = bf16_halves(merges.T)
    section, merges = (np.asarray(x, np.float32) for x in (section.T, merges))
    return section, merges, shares, bf16_halves(spread), bf16_halves(table)


def bf16_halves(x):
    high = x.astype(jnp.bfloat16)
    return high, (x - high.astype(np.float64)).astype(jnp.bfloat16)


def dot(spec, left, right):
    return jnp.einsum(spec, left, right, precision=HIGH, preferred_element_type=jnp.float32)


def halves(x):
    high = x.astype(jnp.bfloat16)
    return high, (x - high.astype(jnp.float32)).astype(jnp.bfloat16)


def mxu(left, right, contract):
    return lax.dot_general(left, right, (contract, ((), ())), preferred_element_type=jnp.float32)


NN = ((1,), (0,))
NT = ((1,), (1,))
TN = ((0,), (0,))


def stacked(left, right, contract):
    rows = left.shape[0]
    high, low = halves(left)
    both = mxu(jnp.concatenate([high, low], axis=0), right[0], contract)
    return both[:rows] + both[rows:] + mxu(high, right[1], contract)


def product(left, right, contract):
    (lh, ll), (rh, rl) = left, right
    return mxu(lh, rh, contract) + mxu(lh, rl, contract) + mxu(ll, rh, contract)


def wide(x):
    return jnp.concatenate(halves(x), axis=1)


def angles(offset, first, total):
    pixel = first + lax.broadcasted_iota(jnp.int32, (1, BC), 1)
    turn = ((2 * offset + (CR - 1)) * pixel) % (2 * total)
    angle = turn.astype(jnp.float32) * (jnp.pi / total)
    return jnp.cos(angle), jnp.sin(angle)


def first_pixel(rows):
    return (lax.axis_index("facet") * lax.axis_size("vis") + lax.axis_index("vis")) * rows


def project_kernel(vises, total, offset_ref, count_ref, id_ref, sky_ref, wt_ref, section_ref, high_ref, low_ref, out_ref, scale_ref, offset_row_ref):
    slots = wt_ref.shape[0]
    slot = lax.broadcasted_iota(jnp.int32, wt_ref.shape, 0)
    scale_ref[...] = jnp.where(slot < count_ref[0], wt_ref[...].astype(jnp.float32), 0.0)
    lane = lax.broadcasted_iota(jnp.int32, (1, BC), 1)
    ids = jnp.zeros((1, BC), jnp.int32)
    for s in range(slots):
        ids = jnp.where(lane == s, id_ref[s], ids)
    offset = jnp.full(offset_row_ref.shape, offset_ref[0], jnp.int32)
    offset_row_ref[...] = offset.astype(jnp.float32)
    cos_p, sin_p = angles(offset_ref[0], first_pixel(sky_ref.shape[0]), total)
    section = section_ref[...]
    into = jnp.concatenate([section * cos_p, -section * sin_p], axis=0)
    coef = stacked(into, halves(sky_ref[...]), NN)
    for v in range(vises):
        both = stacked(coef, (high_ref[v], low_ref[v]), NN)
        out_ref[v, :RANKS, :] = both[:RANKS, :BC] + both[RANKS:, BC:]
        out_ref[v, RANKS:, :] = both[RANKS:, :BC] - both[:RANKS, BC:]
        out_ref[v, SPARE : SPARE + 1, :] = ids.astype(jnp.float32)


def ids_columns(held_ref, vises, slots):
    row = lax.broadcasted_iota(jnp.int32, (slots, BC), 0)
    lane = lax.broadcasted_iota(jnp.int32, (slots, BC), 1)
    columns = []
    for v in range(vises):
        ids = jnp.broadcast_to(held_ref[v, SPARE : SPARE + 1, :], (slots, BC))
        column = jnp.sum(jnp.where(row == lane, ids, 0.0), axis=1, keepdims=True)
        columns.append(jnp.broadcast_to(column, (slots, BC)).astype(jnp.int32))
    return columns


def slot_rows(columns, member, vises, groups):
    rows = []
    for v in range(vises):
        for g in range(groups):
            at = vises * g + member
            rows.append(jnp.broadcast_to(columns[v][at : at + 1], (2 * BR, BC)))
    return jnp.concatenate(rows, axis=0)


def selection(ids, bands):
    inner = lax.broadcasted_iota(jnp.int32, ids.shape, 0) % (2 * BR)
    target = (ids // bands) * (2 * BR) + inner
    lane = lax.broadcasted_iota(jnp.int32, ids.shape, 1)
    pieces = [
        jnp.where(target == lane + part * BC, 1.0, 0.0).astype(jnp.bfloat16)
        for part in range(2 * CR // BC)
    ]
    return jnp.concatenate(pieces, axis=1), ids % bands


def everywhere(x, width):
    step = BC // 2
    while step >= width:
        x = x + pltpu.roll(x, step, 1)
        step //= 2
    return x


def pick_kernel(vises, groups, coef_ref, held_ref, high_ref, low_ref, out_ref):
    width = BC // vises
    coef = wide(coef_ref[...])
    grid = mxu(high_ref[...], coef, NN)
    grid = grid[:, :BC] + grid[:, BC:] + mxu(low_ref[...], coef[:, :BC], NN)
    grid = wide(grid)
    columns = ids_columns(held_ref, vises, vises * groups)
    piece = lax.broadcasted_iota(jnp.int32, (vises * groups * 2 * BR, BC), 1) // width
    total = jnp.zeros((vises * groups * 2 * BR, BC), jnp.float32)
    for member in range(vises):
        hot, band = selection(slot_rows(columns, member, vises, groups), K // BC)
        rows = mxu(hot, grid, NN)
        rows = rows[:, :BC] + rows[:, BC:]
        rows = everywhere(jnp.where(piece == band, rows, 0.0), width)
        total = jnp.where(piece == member, rows, total)
    out_ref[...] = total.reshape(out_ref.shape)


def place_kernel(vises, groups, part_ref, held_ref, high_ref, low_ref, out_ref):
    width = BC // vises
    parts = part_ref[...].reshape(vises * groups * 2 * BR, BC)
    columns = ids_columns(held_ref, vises, vises * groups)
    piece = lax.broadcasted_iota(jnp.int32, parts.shape, 1) // width
    turned = jnp.zeros((2 * BC, 2 * CR), jnp.float32)
    for member in range(vises):
        hot, band = selection(slot_rows(columns, member, vises, groups), K // BC)
        rows = everywhere(jnp.where(piece == member, parts, 0.0), width)
        turned = turned + mxu(wide(jnp.where(piece == band, rows, 0.0)), hot, TN)
    turned = turned[:BC] + turned[BC:]
    coef = stacked(turned, (high_ref[...], low_ref[...]), NN)
    out_ref[...] = coef.T.reshape(out_ref.shape)


def degrid_kernel(vises, groups, got_ref, rows_ref, cols_ref, seen_ref, scale_ref, res_ref, out_ref):
    width = BC // vises
    tall = 2 * BR
    piece = lax.broadcasted_iota(jnp.int32, (tall, BC), 1) // width
    for g in range(groups):
        at = pl.ds(g * tall, tall)
        held = [got_ref[v, at, :] for v in range(vises)]
        backs = []
        for member in range(vises):
            slot = vises * g + member
            block = held[member]
            for v in range(vises):
                if v != member:
                    moved = pltpu.roll(held[v], (width * (v - member)) % BC, 1)
                    block = jnp.where(piece == v, moved, block)
            high, low = halves(cols_ref[slot])
            both = mxu(
                jnp.concatenate(halves(block), axis=0), jnp.concatenate([high, low], axis=1), NN
            )
            along = both[:tall, :BC] + both[:tall, BC:] + both[tall:, :BC]
            weight_rows = rows_ref[slot]
            model = jnp.sum(along.reshape(2, BR, BC) * weight_rows[None], axis=1)
            residual = scale_ref[slot : slot + 1, :] * (seen_ref[slot] - model)
            res_ref[slot] = residual
            out = (weight_rows[None] * residual[:, None, :]).reshape(tall, BC)
            both = mxu(
                jnp.concatenate(halves(out), axis=0), jnp.concatenate([high, low], axis=0), NT
            )
            backs.append(both[:tall, :BC] + both[:tall, BC:] + both[tall:, :BC])
        for v in range(vises):
            sent = backs[v]
            for member in range(vises):
                if member != v:
                    moved = pltpu.roll(backs[member], (width * (member - v)) % BC, 1)
                    sent = jnp.where(piece == member, moved, sent)
            out_ref[v, at, :] = sent


def share_kernel(vises, subs, got_ref, offset_row_ref, high_ref, low_ref, out_ref):
    facet = got_ref[0]
    for f in range(1, got_ref.shape[0]):
        facet = facet + got_ref[f]
    coef = product((high_ref[...], low_ref[...]), halves(facet), NN)
    row = lax.broadcasted_iota(jnp.int32, coef.shape, 0) % (2 * RANKS)
    coef = jnp.where(row == SPARE, offset_row_ref[:1, :], coef)
    coef = coef.reshape(vises, 2 * RANKS, BC)
    for q in range(subs):
        out_ref[q * vises : (q + 1) * vises] = coef


def image_kernel(vises, subs, total, got_ref, section_ref, high_ref, low_ref, out_ref):
    rows = out_ref.shape[0]
    section = section_ref[...]
    first = first_pixel(rows)
    out = []
    coef = []
    for q in range(subs):
        offset = got_ref[q * vises, SPARE : SPARE + 1, :].astype(jnp.int32)
        cos_p, sin_p = angles(offset, first, total)
        cos_p, sin_p = section * cos_p, section * sin_p
        out.append(
            jnp.concatenate(
                [
                    jnp.concatenate([cos_p, -sin_p], axis=1),
                    jnp.concatenate([-sin_p, -cos_p], axis=1),
                ],
                axis=0,
            )
        )
        coef.append(jnp.concatenate([got_ref[q * vises + v] for v in range(vises)], axis=1))
    out_high, out_low = halves(jnp.concatenate(out, axis=0))
    high, low = halves(jnp.concatenate(coef, axis=0))
    grid = mxu(out_high, high, TN) + mxu(out_high, low, TN) + mxu(out_low, high, TN)
    image = jnp.zeros(out_ref.shape, jnp.float32)
    for v in range(vises):
        at = slice(v * BC, (v + 1) * BC)
        part = jnp.concatenate([grid[:rows, at], grid[rows:, at]], axis=1)
        image = image + stacked(part, (high_ref[v], low_ref[v]), NT)
    out_ref[...] = image


def whole():
    return pl.BlockSpec(memory_space=pltpu.VMEM)


def shards(sky, row_offsets, block_counts, block_ids, kernel_rows, kernel_cols, observed, weights):
    facets = lax.axis_size("facet")
    vises = lax.axis_size("vis")
    subs = lax.axis_size("sub")
    total = facets * K
    rows = sky.shape[0]
    lanes = K // vises
    slots = block_ids.shape[0]
    groups = slots // vises
    section, merges, shares, spread, table = constants(facets, vises, total)
    shares = [jnp.asarray(x) for x in shares]
    spread = [jnp.asarray(x) for x in spread]
    table = [jnp.asarray(x) for x in table]

    def call(kernel, name, args, outs, scalars=0):
        smem = pl.BlockSpec(memory_space=pltpu.SMEM)
        specs = tuple(whole() for _ in outs)
        return pl.pallas_call(
            kernel,
            out_shape=tuple(jax.ShapeDtypeStruct(x, jnp.float32) for x in outs),
            in_specs=[smem] * scalars + [whole()] * (len(args) - scalars),
            out_specs=specs,
            compiler_params=pltpu.CompilerParams(vmem_limit_bytes=16 << 20),
            name=name,
        )(*args)

    sent, scale, offset_row = call(
        functools.partial(project_kernel, vises, total),
        "project",
        (row_offsets, block_counts, block_ids, sky, weights, section, *table),
        ((vises, 2 * RANKS, lanes), (slots, BC), (8, lanes)),
        scalars=3,
    )
    held = lax.all_to_all(sent, "vis", 0, 0, tiled=True)
    facet_coef = dot("kx,xl->kl", merges, held.reshape(vises * 2 * RANKS, lanes))
    sent = jnp.broadcast_to(facet_coef[None], (facets, 2 * RANK, lanes))
    got = lax.all_to_all(sent, "facet", 0, 0, tiled=True)

    exchange = (vises, groups * 2 * BR, lanes)
    (sent,) = call(
        functools.partial(pick_kernel, vises, groups),
        "pick",
        (got.reshape(facets * 2 * RANK, lanes), held, *spread),
        (exchange,),
    )
    got = lax.all_to_all(sent, "vis", 0, 0, tiled=True)
    residual, sent = call(
        functools.partial(degrid_kernel, vises, groups),
        "degrid",
        (got, kernel_rows, kernel_cols, observed, scale),
        ((slots, 2, BC), exchange),
    )
    got = lax.all_to_all(sent, "vis", 0, 0, tiled=True)
    (sent,) = call(
        functools.partial(place_kernel, vises, groups),
        "place",
        (got, held, *spread),
        ((facets, 2 * RANK, lanes),),
    )
    got = lax.all_to_all(sent, "facet", 0, 0, tiled=True)

    (sent,) = call(
        functools.partial(share_kernel, vises, subs),
        "share",
        (got, offset_row, *shares),
        ((subs * vises, 2 * RANKS, lanes),),
    )
    got = lax.all_to_all(sent, ("sub", "vis"), 0, 0, tiled=True)
    (image,) = call(
        functools.partial(image_kernel, vises, subs, total),
        "image",
        (got, section, *table),
        ((rows, K),),
    )
    return (image, residual)


def solution(mesh):
    return jax.shard_map(
        shards,
        mesh=mesh,
        in_specs=(
            P(("facet", "vis"), None),
            P("sub"),
            P(("facet", "sub", "vis")),
            P(("facet", "sub", "vis")),
            P(("facet", "sub", "vis"), None, None),
            P(("facet", "sub", "vis"), None, None),
            P(("facet", "sub", "vis"), None, None),
            P(("facet", "sub", "vis"), None),
        ),
        out_specs=(P(("facet", "vis"), None), P(("facet", "sub", "vis"), None, None)),
        check_vma=False,
    )
```

```python
import functools

import jax
import jax.numpy as jnp
import numpy as np
from jax import lax
from jax.experimental import pallas as pl
from jax.experimental.pallas import tpu as pltpu
from jax.sharding import PartitionSpec as P

K = 512
CR = 256
BR = 8
BC = 128
SUBS = 8
RANK = 28
RANKS = 16
SPARE = RANKS - 1


def prolate(count, band, total, rank):
    j = np.arange(count, dtype=np.float64)
    diag = -np.cos(np.pi * (2 * j - count + 1) / total) * np.cos(np.pi * band / total)
    m = np.arange(1, count, dtype=np.float64)
    off = np.sin(np.pi * m / total) * np.sin(np.pi * (count - m) / total)
    values, vectors = np.linalg.eigh(np.diag(diag) + np.diag(off, 1) + np.diag(off, -1))
    basis = vectors[:, ::-1][:, :rank]
    signs = np.sign(np.sum(basis[count // 2 :], axis=0))
    return basis * signs


def constants(facets, vises, total):
    rows = K // vises
    lanes = K // vises
    basis = prolate(K, CR, total, RANK)
    section = prolate(rows, CR, total, RANKS)
    section[:, SPARE] = 0.0
    merge = np.stack([section.T @ basis[v * rows : (v + 1) * rows] for v in range(vises)])
    r = np.arange(CR) - (CR - 1) / 2
    p = np.arange(K) - (K - 1) / 2
    kernel = np.exp(-2j * np.pi * np.outer(r, p) / total) @ basis
    centres = np.arange(facets) * K + (K - 1) / 2
    shift = np.exp(-2j * np.pi * np.outer(r, centres) / total)
    expand = shift[:, :, None] * kernel[:, None, :] * total**-0.5
    real, imag = expand.real, expand.imag
    spread = np.stack(
        [np.stack([real, -imag], axis=2), np.stack([imag, real], axis=2)], axis=0
    )
    spread = spread.reshape(2, CR // BR, BR, facets * 2 * RANK).transpose(1, 0, 2, 3)
    spread = spread.reshape(2 * CR, facets * 2 * RANK)
    merges = np.zeros((2, RANK, vises, 2, RANKS))
    for part in range(2):
        merges[part, :, :, part, :] = merge.transpose(2, 0, 1)
    merges = merges.reshape(2 * RANK, vises * 2 * RANKS)
    angle = 2 * np.pi * (np.outer(np.arange(lanes), np.arange(lanes)) % lanes) / lanes
    table = np.concatenate([np.cos(angle), np.sin(angle)], axis=1) * K**-0.5
    twist = 2 * np.pi * np.outer(np.arange(vises), np.arange(lanes)) / K
    twist = np.concatenate([np.cos(twist), np.sin(twist)], axis=0).astype(np.float32)
    shares = bf16_halves(merges.T)
    section, merges = (np.asarray(x, np.float32) for x in (section.T, merges))
    return section, merges, shares, np.stack(bf16_halves(spread)), bf16_halves(table), twist


def bf16_halves(x):
    high = x.astype(jnp.bfloat16)
    return high, (x - high.astype(np.float64)).astype(jnp.bfloat16)


def halves(x):
    high = x.astype(jnp.bfloat16)
    return high, (x - high.astype(jnp.float32)).astype(jnp.bfloat16)


def mxu(left, right, contract):
    return lax.dot_general(left, right, (contract, ((), ())), preferred_element_type=jnp.float32)


NN = ((1,), (0,))
NT = ((1,), (1,))
TN = ((0,), (0,))


def stacked(left, right, contract):
    rows = left.shape[0]
    high, low = halves(left)
    both = mxu(jnp.concatenate([high, low], axis=0), right[0], contract)
    return both[:rows] + both[rows:] + mxu(high, right[1], contract)


def product(left, right, contract):
    (lh, ll), (rh, rl) = left, right
    return mxu(lh, rh, contract) + mxu(lh, rl, contract) + mxu(ll, rh, contract)


def wide(x):
    return jnp.concatenate(halves(x), axis=1)


def angles(offset, first, total):
    pixel = first + lax.broadcasted_iota(jnp.int32, (1, BC), 1)
    turn = ((2 * offset + (CR - 1)) * pixel) % (2 * total)
    angle = turn.astype(jnp.float32) * (jnp.pi / total)
    return jnp.cos(angle), jnp.sin(angle)


def first_pixel(rows):
    return (lax.axis_index("facet") * lax.axis_size("vis") + lax.axis_index("vis")) * rows


def project_kernel(vises, total, *refs):
    sources, rest = refs[:9], refs[9:]
    out_ref, scale_ref, offset_row_ref = rest[:3]
    targets, sem = rest[3:12], rest[12]
    copies = [
        pltpu.make_async_copy(source, target, sem.at[n])
        for n, (source, target) in enumerate(zip(sources, targets))
    ]
    for copy in copies:
        copy.start()
    for copy in copies:
        copy.wait()
    offset_ref, count_ref, id_ref, section_ref, twist_ref, sky_ref, high_ref, low_ref, wt_ref = targets
    slots = wt_ref.shape[0]
    slot = lax.broadcasted_iota(jnp.int32, wt_ref.shape, 0)
    scale_ref[...] = jnp.where(slot < count_ref[0], wt_ref[...].astype(jnp.float32), 0.0)
    lane = lax.broadcasted_iota(jnp.int32, (1, BC), 1)
    ids = jnp.zeros((1, BC), jnp.int32)
    for s in range(slots):
        ids = jnp.where(lane == s, id_ref[s], ids)
    offset = jnp.full(offset_row_ref.shape, offset_ref[0], jnp.int32)
    offset_row_ref[...] = offset.astype(jnp.float32)
    cos_p, sin_p = angles(offset_ref[0], first_pixel(sky_ref.shape[0]), total)
    section = section_ref[...]
    into = jnp.concatenate([section * cos_p, -section * sin_p], axis=0)
    coef = stacked(into, halves(sky_ref[...]), NN)
    real, imag = [], []
    for k in range(vises):
        real.append(coef[:RANKS, k * BC : (k + 1) * BC])
        imag.append(coef[RANKS:, k * BC : (k + 1) * BC])
    re_e, re_o = real[0] + real[2], real[1] + real[3]
    im_e, im_o = imag[0] + imag[2], imag[1] + imag[3]
    re_d, re_g = real[0] - real[2], real[1] - real[3]
    im_d, im_g = imag[0] - imag[2], imag[1] - imag[3]
    folded = [
        (re_e + re_o, im_e + im_o),
        (re_d + im_g, im_d - re_g),
        (re_e - re_o, im_e - im_o),
        (re_d - im_g, im_d + re_g),
    ]
    rows = []
    for v, (re, im) in enumerate(folded):
        cos_t, sin_t = twist_ref[v : v + 1, :], twist_ref[vises + v : vises + v + 1, :]
        rows += [re * cos_t + im * sin_t, im * cos_t - re * sin_t]
    both = stacked(jnp.concatenate(rows, axis=0), (high_ref[...], low_ref[...]), NN)
    for v in range(vises):
        re = both[2 * v * RANKS : (2 * v + 1) * RANKS]
        im = both[(2 * v + 1) * RANKS : (2 * v + 2) * RANKS]
        out_ref[v, :RANKS, :] = re[:, :BC] + im[:, BC:]
        out_ref[v, RANKS:, :] = im[:, :BC] - re[:, BC:]
        out_ref[v, SPARE : SPARE + 1, :] = ids.astype(jnp.float32)


def ids_columns(held_ref, vises, slots):
    row = lax.broadcasted_iota(jnp.int32, (slots, BC), 0)
    lane = lax.broadcasted_iota(jnp.int32, (slots, BC), 1)
    columns = []
    for v in range(vises):
        ids = jnp.broadcast_to(held_ref[v, SPARE : SPARE + 1, :], (slots, BC))
        column = jnp.sum(jnp.where(row == lane, ids, 0.0), axis=1, keepdims=True)
        columns.append(jnp.broadcast_to(column, (slots, BC)).astype(jnp.int32))
    return columns


def slot_rows(columns, member, vises, groups):
    rows = []
    for v in range(vises):
        for g in range(groups):
            at = vises * g + member
            rows.append(jnp.broadcast_to(columns[v][at : at + 1], (2 * BR, BC)))
    return jnp.concatenate(rows, axis=0)


def selection(ids, bands):
    inner = lax.broadcasted_iota(jnp.int32, ids.shape, 0) % (2 * BR)
    target = (ids // bands) * (2 * BR) + inner
    lane = lax.broadcasted_iota(jnp.int32, ids.shape, 1)
    pieces = [
        jnp.where(target == lane + part * BC, 1.0, 0.0).astype(jnp.bfloat16)
        for part in range(2 * CR // BC)
    ]
    return jnp.concatenate(pieces, axis=1), ids % bands


def everywhere(x, width):
    step = BC // 2
    while step >= width:
        x = x + pltpu.roll(x, step, 1)
        step //= 2
    return x


def pick_kernel(vises, groups, coef_ref, held_ref, spread_ref, out_ref):
    width = BC // vises
    coef = wide(coef_ref[...])
    grid = mxu(spread_ref[0], coef, NN)
    grid = grid[:, :BC] + grid[:, BC:] + mxu(spread_ref[1], coef[:, :BC], NN)
    grid = wide(grid)
    columns = ids_columns(held_ref, vises, vises * groups)
    piece = lax.broadcasted_iota(jnp.int32, (vises * groups * 2 * BR, BC), 1) // width
    total = jnp.zeros((vises * groups * 2 * BR, BC), jnp.float32)
    for member in range(vises):
        hot, band = selection(slot_rows(columns, member, vises, groups), K // BC)
        rows = mxu(hot, grid, NN)
        rows = rows[:, :BC] + rows[:, BC:]
        rows = everywhere(jnp.where(piece == band, rows, 0.0), width)
        total = jnp.where(piece == member, rows, total)
    out_ref[...] = total.reshape(out_ref.shape)


def place_kernel(vises, groups, part_ref, held_ref, spread_ref, out_ref):
    width = BC // vises
    parts = part_ref[...].reshape(vises * groups * 2 * BR, BC)
    columns = ids_columns(held_ref, vises, vises * groups)
    piece = lax.broadcasted_iota(jnp.int32, parts.shape, 1) // width
    turned = jnp.zeros((2 * BC, 2 * CR), jnp.float32)
    for member in range(vises):
        hot, band = selection(slot_rows(columns, member, vises, groups), K // BC)
        rows = everywhere(jnp.where(piece == member, parts, 0.0), width)
        turned = turned + mxu(wide(jnp.where(piece == band, rows, 0.0)), hot, TN)
    turned = turned[:BC] + turned[BC:]
    coef = stacked(turned, (spread_ref[0], spread_ref[1]), NN)
    out_ref[...] = coef.T.reshape(out_ref.shape)


def degrid_kernel(vises, groups, got_ref, rows_ref, cols_ref, seen_ref, scale_ref, res_ref, out_ref):
    width = BC // vises
    tall = 2 * BR
    piece = lax.broadcasted_iota(jnp.int32, (tall, BC), 1) // width
    for g in range(groups):
        at = pl.ds(g * tall, tall)
        held = [got_ref[v, at, :] for v in range(vises)]
        backs = []
        for member in range(vises):
            slot = vises * g + member
            block = held[member]
            for v in range(vises):
                if v != member:
                    moved = pltpu.roll(held[v], (width * (v - member)) % BC, 1)
                    block = jnp.where(piece == v, moved, block)
            cols = [cols_ref[slot, pl.ds(v, width, stride=vises), :] for v in range(vises)]
            high, low = halves(jnp.concatenate(cols, axis=0))
            both = mxu(
                jnp.concatenate(halves(block), axis=0), jnp.concatenate([high, low], axis=1), NN
            )
            along = both[:tall, :BC] + both[:tall, BC:] + both[tall:, :BC]
            weight_rows = rows_ref[slot]
            model = jnp.sum(along.reshape(2, BR, BC) * weight_rows[None], axis=1)
            residual = scale_ref[slot : slot + 1, :] * (seen_ref[slot] - model)
            res_ref[slot] = residual
            out = (weight_rows[None] * residual[:, None, :]).reshape(tall, BC)
            both = mxu(
                jnp.concatenate(halves(out), axis=0), jnp.concatenate([high, low], axis=0), NT
            )
            backs.append(both[:tall, :BC] + both[:tall, BC:] + both[tall:, :BC])
        for v in range(vises):
            sent = backs[v]
            for member in range(vises):
                if member != v:
                    moved = pltpu.roll(backs[member], (width * (member - v)) % BC, 1)
                    sent = jnp.where(piece == member, moved, sent)
            out_ref[v, at, :] = sent


def share_kernel(vises, subs, got_ref, offset_row_ref, high_ref, low_ref, out_ref):
    facet = got_ref[0]
    for f in range(1, got_ref.shape[0]):
        facet = facet + got_ref[f]
    coef = product((high_ref[...], low_ref[...]), halves(facet), NN)
    row = lax.broadcasted_iota(jnp.int32, coef.shape, 0) % (2 * RANKS)
    coef = jnp.where(row == SPARE, offset_row_ref[:1, :], coef)
    coef = coef.reshape(vises, 2 * RANKS, BC)
    for q in range(subs):
        out_ref[q * vises : (q + 1) * vises] = coef


def image_kernel(vises, subs, total, got_ref, section_ref, twist_ref, high_ref, low_ref, out_ref):
    rows = out_ref.shape[0]
    section = section_ref[...]
    first = first_pixel(rows)
    out = []
    coef = []
    for q in range(subs):
        offset = got_ref[q * vises, SPARE : SPARE + 1, :].astype(jnp.int32)
        cos_p, sin_p = angles(offset, first, total)
        cos_p, sin_p = section * cos_p, section * sin_p
        out.append(
            jnp.concatenate(
                [
                    jnp.concatenate([cos_p, -sin_p], axis=1),
                    jnp.concatenate([-sin_p, -cos_p], axis=1),
                ],
                axis=0,
            )
        )
        coef.append(jnp.concatenate([got_ref[q * vises + v] for v in range(vises)], axis=1))
    out_high, out_low = halves(jnp.concatenate(out, axis=0))
    high, low = halves(jnp.concatenate(coef, axis=0))
    grid = mxu(out_high, high, TN) + mxu(out_high, low, TN) + mxu(out_low, high, TN)
    real, imag = [], []
    for v in range(vises):
        both = stacked(grid[:, v * BC : (v + 1) * BC], (high_ref[...], low_ref[...]), NN)
        re = both[:rows, :BC] + both[rows:, BC:]
        im = both[:rows, BC:] - both[rows:, :BC]
        cos_t, sin_t = twist_ref[v : v + 1, :], twist_ref[vises + v : vises + v + 1, :]
        real.append(re * cos_t - im * sin_t)
        imag.append(re * sin_t + im * cos_t)
    even, odd = real[0] + real[2], real[1] + real[3]
    flat, turn = real[0] - real[2], imag[3] - imag[1]
    for k, part in enumerate((even + odd, flat + turn, even - odd, flat - turn)):
        out_ref[:, k * BC : (k + 1) * BC] = part


def whole():
    return pl.BlockSpec(memory_space=pltpu.VMEM)


def shards(sky, row_offsets, block_counts, block_ids, kernel_rows, kernel_cols, observed, weights):
    facets = lax.axis_size("facet")
    vises = lax.axis_size("vis")
    subs = lax.axis_size("sub")
    total = facets * K
    rows = sky.shape[0]
    lanes = K // vises
    slots = block_ids.shape[0]
    groups = slots // vises
    section, merges, shares, spread, table, twist = constants(facets, vises, total)
    shares = [jnp.asarray(x) for x in shares]
    spread = jnp.asarray(spread)
    table = [jnp.asarray(x) for x in table]

    def call(kernel, name, args, outs):
        specs = tuple(whole() for _ in outs)
        return pl.pallas_call(
            kernel,
            out_shape=tuple(jax.ShapeDtypeStruct(x, jnp.float32) for x in outs),
            in_specs=[whole()] * len(args),
            out_specs=specs,
            compiler_params=pltpu.CompilerParams(vmem_limit_bytes=16 << 20),
            name=name,
        )(*args)

    args = (row_offsets, block_counts, block_ids, section, twist, sky, *table, weights)
    sent, scale, offset_row = pl.pallas_call(
        functools.partial(project_kernel, vises, total),
        out_shape=tuple(
            jax.ShapeDtypeStruct(x, jnp.float32)
            for x in ((vises, 2 * RANKS, lanes), (slots, BC), (8, lanes))
        ),
        in_specs=[pl.BlockSpec(memory_space=pltpu.HBM)] * len(args),
        out_specs=(whole(), whole(), whole()),
        scratch_shapes=[
            (pltpu.SMEM if n < 3 else pltpu.VMEM)(x.shape, x.dtype) for n, x in enumerate(args)
        ]
        + [pltpu.SemaphoreType.DMA((len(args),))],
        compiler_params=pltpu.CompilerParams(vmem_limit_bytes=123 << 19),
        name="project",
    )(*args)
    held = lax.all_to_all(sent, "vis", 0, 0, tiled=True)
    facet_coef = jnp.dot(
        merges,
        held.reshape(vises * 2 * RANKS, lanes),
        precision=lax.Precision.HIGH,
        preferred_element_type=jnp.float32,
    )
    sent = jnp.broadcast_to(facet_coef[None], (facets, 2 * RANK, lanes))
    got = lax.all_to_all(sent, "facet", 0, 0, tiled=True)

    exchange = (vises, groups * 2 * BR, lanes)
    (sent,) = call(
        functools.partial(pick_kernel, vises, groups),
        "pick",
        (got.reshape(facets * 2 * RANK, lanes), held, spread),
        (exchange,),
    )
    got = lax.all_to_all(sent, "vis", 0, 0, tiled=True)
    residual, sent = call(
        functools.partial(degrid_kernel, vises, groups),
        "degrid",
        (got, kernel_rows, kernel_cols, observed, scale),
        ((slots, 2, BC), exchange),
    )
    got = lax.all_to_all(sent, "vis", 0, 0, tiled=True)
    (sent,) = call(
        functools.partial(place_kernel, vises, groups),
        "place",
        (got, held, spread),
        ((facets, 2 * RANK, lanes),),
    )
    got = lax.all_to_all(sent, "facet", 0, 0, tiled=True)

    (sent,) = call(
        functools.partial(share_kernel, vises, subs),
        "share",
        (got, offset_row, *shares),
        ((subs * vises, 2 * RANKS, lanes),),
    )
    got = lax.all_to_all(sent, ("sub", "vis"), 0, 0, tiled=True)
    (image,) = call(
        functools.partial(image_kernel, vises, subs, total),
        "image",
        (got, section, twist, *table),
        ((rows, K),),
    )
    return (image, residual)


def solution(mesh):
    return jax.shard_map(
        shards,
        mesh=mesh,
        in_specs=(
            P(("facet", "vis"), None),
            P("sub"),
            P(("facet", "sub", "vis")),
            P(("facet", "sub", "vis")),
            P(("facet", "sub", "vis"), None, None),
            P(("facet", "sub", "vis"), None, None),
            P(("facet", "sub", "vis"), None, None),
            P(("facet", "sub", "vis"), None),
        ),
        out_specs=(P(("facet", "vis"), None), P(("facet", "sub", "vis"), None, None)),
        check_vma=False,
    )
```

```python
import functools

import jax
import jax.numpy as jnp
import numpy as np
from jax import lax
from jax.experimental import pallas as pl
from jax.experimental.pallas import tpu as pltpu
from jax.sharding import PartitionSpec as P

K = 512
CR = 256
BR = 8
BC = 128
SUBS = 8
RANK = 28
NEAR = 4
GROUP_RANK = 80
RANKS = 16
SPARE = RANKS - 1


def prolate(count, band, total, rank):
    j = np.arange(count, dtype=np.float64)
    diag = -np.cos(np.pi * (2 * j - count + 1) / total) * np.cos(np.pi * band / total)
    m = np.arange(1, count, dtype=np.float64)
    off = np.sin(np.pi * m / total) * np.sin(np.pi * (count - m) / total)
    values, vectors = np.linalg.eigh(np.diag(diag) + np.diag(off, 1) + np.diag(off, -1))
    basis = vectors[:, ::-1][:, :rank]
    signs = np.sign(np.sum(basis[count // 2 :], axis=0))
    return basis * signs


def constants(facets, vises, total):
    rows = K // vises
    lanes = K // vises
    basis = prolate(K, CR, total, RANK)
    section = prolate(rows, CR, total, RANKS)
    section[:, SPARE] = 0.0
    merge = np.stack([section.T @ basis[v * rows : (v + 1) * rows] for v in range(vises)])
    r = np.arange(CR) - (CR - 1) / 2
    p = np.arange(K) - (K - 1) / 2
    kernel = np.exp(-2j * np.pi * np.outer(r, p) / total) @ basis
    centres = np.arange(facets) * K + (K - 1) / 2
    shift = np.exp(-2j * np.pi * np.outer(r, centres) / total)
    expand = shift[:, :, None] * kernel[:, None, :] * total**-0.5
    real, imag = expand.real, expand.imag
    spread = np.stack(
        [np.stack([real, -imag], axis=2), np.stack([imag, real], axis=2)], axis=0
    )
    spread = spread.reshape(2, CR // BR, BR, facets * 2 * RANK).transpose(1, 0, 2, 3)
    spread = spread.reshape(2 * CR, facets * 2 * RANK)
    merges = np.zeros((2, RANK, vises, 2, RANKS))
    for part in range(2):
        merges[part, :, :, part, :] = merge.transpose(2, 0, 1)
    merges = merges.reshape(2 * RANK, vises * 2 * RANKS)
    span = NEAR * K
    wide_basis = prolate(span, CR, total, GROUP_RANK)
    joins = np.zeros((4, GROUP_RANK, NEAR * vises, 8))
    for n in range(NEAR * vises):
        join = section.T @ wide_basis[n * rows : (n + 1) * rows]
        for j in range(4):
            joins[j, :, n] = join[8 * (j % 2) : 8 * (j % 2) + 8].T
    joins = np.stack(bf16_halves(joins.reshape(4 * GROUP_RANK, NEAR * vises * 8)))
    p = np.arange(span) - (span - 1) / 2
    kernel = np.exp(-2j * np.pi * np.outer(r, p) / total) @ wide_basis
    centres = np.arange(facets // NEAR) * span + (span - 1) / 2
    shift = np.exp(-2j * np.pi * np.outer(r, centres) / total)
    expand = shift[:, :, None] * kernel[:, None, :] * total**-0.5
    real, imag = expand.real, expand.imag
    grow = np.stack(
        [np.stack([real, -imag], axis=2), np.stack([imag, real], axis=2)], axis=0
    )
    quarter = 2 * GROUP_RANK // 4
    grow = grow.reshape(2, CR // BR, BR, facets // NEAR, 4, quarter)
    grow = grow.transpose(0, 2, 1, 4, 3, 5).reshape(2 * CR, facets // NEAR * 2 * GROUP_RANK)
    grow = np.stack(bf16_halves(grow))

    def column_table(order):
        angle = 2 * np.pi * (np.outer(np.arange(lanes), order) % lanes) / lanes
        return np.cos(angle) * K**-0.5, np.sin(angle) * K**-0.5

    index = np.arange(lanes)
    out_order = 32 * (index // 8 % 4) + 8 * (index // 32) + index % 8
    back_order = 32 * (index % 4) + index // 4
    table = bf16_halves(np.concatenate(column_table(out_order), axis=1))
    back_table = bf16_halves(np.concatenate([x.T for x in column_table(back_order)], axis=1))
    twist = 2 * np.pi * np.outer(np.arange(vises), np.arange(lanes)) / K
    twist = np.concatenate([np.cos(twist), np.sin(twist)], axis=0).astype(np.float32)
    shares = bf16_halves(merges.T)
    section = np.asarray(section.T, np.float32)
    spread = np.stack(bf16_halves(spread))
    return section, joins, grow, shares, spread, table, back_table, twist


def bf16_halves(x):
    high = x.astype(jnp.bfloat16)
    return high, (x - high.astype(np.float64)).astype(jnp.bfloat16)


def halves(x):
    high = x.astype(jnp.bfloat16)
    return high, (x - high.astype(jnp.float32)).astype(jnp.bfloat16)


def mxu(left, right, contract):
    return lax.dot_general(left, right, (contract, ((), ())), preferred_element_type=jnp.float32)


NN = ((1,), (0,))
NT = ((1,), (1,))
TN = ((0,), (0,))


def stacked(left, right, contract):
    rows = left.shape[0]
    high, low = halves(left)
    both = mxu(jnp.concatenate([high, low], axis=0), right[0], contract)
    return both[:rows] + both[rows:] + mxu(high, right[1], contract)


def product(left, right, contract):
    (lh, ll), (rh, rl) = left, right
    return mxu(lh, rh, contract) + mxu(lh, rl, contract) + mxu(ll, rh, contract)


def wide(x):
    return jnp.concatenate(halves(x), axis=1)


def angles(offset, first, total):
    pixel = first + lax.broadcasted_iota(jnp.int32, (1, BC), 1)
    turn = ((2 * offset + (CR - 1)) * pixel) % (2 * total)
    angle = turn.astype(jnp.float32) * (jnp.pi / total)
    return jnp.cos(angle), jnp.sin(angle)


def near_index():
    return lax.axis_index("zl")


def first_pixel(rows):
    facet = lax.axis_index("zh") * NEAR + near_index()
    return (facet * lax.axis_size("vis") + lax.axis_index("vis")) * rows


def exchanged(arrays, pairs):
    lane = lax.broadcasted_iota(jnp.int32, arrays[0].shape, 1)
    for step, size in pairs:
        upper = (lane // size) % 2 == 1
        after = list(arrays)
        for low in range(len(arrays)):
            if (low // step) % 2 == 0:
                one, two = arrays[low], arrays[low + step]
                after[low] = jnp.where(upper, pltpu.roll(two, size, 1), one)
                after[low + step] = jnp.where(upper, two, pltpu.roll(one, BC - size, 1))
        arrays = after
    return arrays


def project_kernel(vises, total, *refs):
    sources, rest = refs[:9], refs[9:]
    out_ref, scale_ref, offset_row_ref = rest[:3]
    targets, sem = rest[3:12], rest[12]
    copies = [
        pltpu.make_async_copy(source, target, sem.at[n])
        for n, (source, target) in enumerate(zip(sources, targets))
    ]
    for copy in copies:
        copy.start()
    for copy in copies:
        copy.wait()
    offset_ref, count_ref, id_ref, section_ref, twist_ref, sky_ref, high_ref, low_ref, wt_ref = targets
    slots = wt_ref.shape[0]
    slot = lax.broadcasted_iota(jnp.int32, wt_ref.shape, 0)
    scale_ref[...] = jnp.where(slot < count_ref[0], wt_ref[...].astype(jnp.float32), 0.0)
    lane = lax.broadcasted_iota(jnp.int32, (1, BC), 1)
    ids = jnp.zeros((1, BC), jnp.int32)
    for s in range(slots):
        ids = jnp.where((lane // 32 == s // 4) & (lane % 4 == s % 4), id_ref[s], ids)
    offset = jnp.full(offset_row_ref.shape, offset_ref[0], jnp.int32)
    offset_row_ref[...] = offset.astype(jnp.float32)
    cos_p, sin_p = angles(offset_ref[0], first_pixel(sky_ref.shape[0]), total)
    section = section_ref[...]
    into = jnp.concatenate([section * cos_p, -section * sin_p], axis=0)
    coef = stacked(into, halves(sky_ref[...]), NN)
    real, imag = [], []
    for k in range(vises):
        real.append(coef[:RANKS, k * BC : (k + 1) * BC])
        imag.append(coef[RANKS:, k * BC : (k + 1) * BC])
    re_e, re_o = real[0] + real[2], real[1] + real[3]
    im_e, im_o = imag[0] + imag[2], imag[1] + imag[3]
    re_d, re_g = real[0] - real[2], real[1] - real[3]
    im_d, im_g = imag[0] - imag[2], imag[1] - imag[3]
    folded = [
        (re_e + re_o, im_e + im_o),
        (re_d + im_g, im_d - re_g),
        (re_e - re_o, im_e - im_o),
        (re_d - im_g, im_d + re_g),
    ]
    rows = []
    for v, (re, im) in enumerate(folded):
        cos_t, sin_t = twist_ref[v : v + 1, :], twist_ref[vises + v : vises + v + 1, :]
        rows += [re * cos_t + im * sin_t, im * cos_t - re * sin_t]
    both = stacked(jnp.concatenate(rows, axis=0), (high_ref[...], low_ref[...]), NN)
    ids = jnp.broadcast_to(ids.astype(jnp.float32), (8, BC))
    chunk = lax.broadcasted_iota(jnp.int32, (8, BC), 1) // 32
    for v in range(vises):
        re = both[2 * v * RANKS : (2 * v + 1) * RANKS]
        im = both[(2 * v + 1) * RANKS : (2 * v + 2) * RANKS]
        rows = jnp.concatenate([re[:, :BC] + im[:, BC:], im[:, :BC] - re[:, BC:]], axis=0)
        for near in range(NEAR):
            packed = jnp.zeros((8, BC), jnp.float32)
            for j in range(4):
                moved = pltpu.roll(rows[8 * j : 8 * j + 8], (32 * (j - near)) % BC, 1)
                packed = jnp.where(chunk == j, moved, packed)
            out_ref[near * vises + v, :8, :] = packed
            out_ref[near * vises + v, 8:, :] = ids


def ids_columns(held_ref, vises, slots):
    row = lax.broadcasted_iota(jnp.int32, (slots, BC), 0)
    lane = lax.broadcasted_iota(jnp.int32, (slots, BC), 1)
    mine = (lane // 32 == row // 4) & (lane % 32 == row % 4)
    columns = []
    for v in range(vises):
        ids = held_ref[near_index() * vises + v, 8:, :]
        ids = jnp.concatenate([ids] * (slots // 8), axis=0)
        column = jnp.sum(jnp.where(mine, ids, 0.0), axis=1, keepdims=True)
        columns.append(jnp.broadcast_to(column, (slots, BC)).astype(jnp.int32))
    return columns


def slot_rows(columns, member, vises, groups):
    rows = []
    for v in range(vises):
        for g in range(groups):
            at = vises * g + member
            rows.append(jnp.broadcast_to(columns[v][at : at + 1], (2 * BR, BC)))
    return jnp.concatenate(rows, axis=0)


def selection(ids, bands):
    inner = lax.broadcasted_iota(jnp.int32, ids.shape, 0) % (2 * BR)
    target = (ids // bands) * (2 * BR) + inner
    lane = lax.broadcasted_iota(jnp.int32, ids.shape, 1)
    pieces = [
        jnp.where(target == lane + part * BC, 1.0, 0.0).astype(jnp.bfloat16)
        for part in range(2 * CR // BC)
    ]
    return jnp.concatenate(pieces, axis=1), ids % bands


def everywhere(x, width):
    step = BC // 2
    while step >= width:
        x = x + pltpu.roll(x, step, 1)
        step //= 2
    return x


def join_kernel(held_ref, joins_ref, out_ref):
    held = wide(held_ref[:, :8, :].reshape(joins_ref.shape[2], BC))
    rows = mxu(joins_ref[0], held, NN)
    rows = rows[:, :BC] + rows[:, BC:] + mxu(joins_ref[1], held[:, :BC], NN)
    half = GROUP_RANK // 2
    chunk = lax.broadcasted_iota(jnp.int32, (half, BC), 1) // 32
    packed = jnp.zeros((half, BC), jnp.float32)
    for part in range(2):
        at = 2 * part * GROUP_RANK
        one, two = rows[at : at + GROUP_RANK], rows[at + GROUP_RANK : at + 2 * GROUP_RANK]
        low = one[:half] + pltpu.roll(two[:half], BC - 32, 1)
        high = pltpu.roll(one[half:], 32, 1) + two[half:]
        packed = jnp.where(chunk == 2 * part, low, packed)
        packed = jnp.where(chunk == 2 * part + 1, high, packed)
    for f in range(out_ref.shape[0]):
        out_ref[f] = packed


def pick_kernel(peers, got_ref, held_ref, grow_ref, out_ref, turned_ref):
    rows = got_ref[...].reshape(got_ref.shape[0] * got_ref.shape[1], BC)
    chunk = lax.broadcasted_iota(jnp.int32, rows.shape, 1) // 32
    coef = [everywhere(jnp.where(chunk == j, rows, 0.0), 32) for j in range(4)]
    coef = wide(jnp.concatenate(coef, axis=0))
    grid = mxu(grow_ref[0], coef, NN)
    grid = grid[:, :BC] + grid[:, BC:] + mxu(grow_ref[1], coef[:, :BC], NN)
    tall, bands = 2 * BR, CR // BR
    moved = [grid] + [pltpu.roll(grid, 8 * d, 1) for d in range(1, 4)]
    eighth = lax.broadcasted_iota(jnp.int32, (bands, BC), 1) // 8
    blocks = []
    for band in range(4):
        block = jnp.zeros((bands, BC), jnp.float32)
        for zr in range(tall):
            source = moved[(zr - band) % 4][zr * bands : (zr + 1) * bands]
            block = jnp.where(eighth == zr, source, block)
        blocks.append(block)
    blocks = wide(jnp.concatenate(blocks, axis=0))
    lane = lax.broadcasted_iota(jnp.int32, (8, BC), 1)
    row = lax.broadcasted_iota(jnp.int32, (BC, BC), 0)
    hots = []
    for top in range(peers // 8):
        ids = jnp.zeros((8, BC), jnp.float32)
        for low in range(8):
            ids = jnp.where((lane // 4) % 8 == low, held_ref[8 * top + low, 8:, :], ids)
        ids = ids.astype(jnp.int32)
        target = (ids % 4) * bands + ids // 4
        target = jnp.broadcast_to(target[:1], (BC, BC))
        hots.append(jnp.where(row == target, 1.0, 0.0).astype(jnp.bfloat16))
    picked = mxu(blocks, jnp.concatenate(hots, axis=1), TN)
    picked = picked[:BC] + picked[BC:]
    for top in range(peers // 8):
        turned_ref[top * BC : (top + 1) * BC, :] = picked[:, top * BC : (top + 1) * BC]
    for top in range(peers // 8):
        parts = [turned_ref[pl.ds(top * BC + i, tall, stride=8), :] for i in range(8)]
        for low, part in enumerate(exchanged(parts, ((1, 4), (2, 8), (4, 16)))):
            out_ref[8 * top + low] = part


def place_kernel(vises, groups, part_ref, held_ref, spread_ref, out_ref):
    parts = part_ref[...].reshape(vises * groups * 2 * BR, BC)
    columns = ids_columns(held_ref, vises, vises * groups)
    piece = lax.broadcasted_iota(jnp.int32, parts.shape, 1) % vises
    turned = jnp.zeros((2 * BC, 2 * CR), jnp.float32)
    for member in range(vises):
        hot, band = selection(slot_rows(columns, member, vises, groups), K // BC)
        alone = jnp.where(piece == member, parts, 0.0)
        rows = alone
        for v in range(vises):
            if v != member:
                rows = rows + pltpu.roll(alone, (v - member) % BC, 1)
        turned = turned + mxu(wide(jnp.where(piece == band, rows, 0.0)), hot, TN)
    turned = turned[:BC] + turned[BC:]
    coef = stacked(turned, (spread_ref[0], spread_ref[1]), NN)
    out_ref[...] = coef.T.reshape(out_ref.shape)


def degrid_kernel(vises, groups, got_ref, rows_ref, cols_ref, seen_ref, scale_ref, res_ref, out_ref):
    tall = 2 * BR
    slots = [got_ref[o] for o in range(got_ref.shape[0])]
    slots = exchanged(slots, ((8, 64), (4, 32), (2, 2), (1, 1)))
    for g in range(groups):
        at = pl.ds(g * tall, tall)
        backs = []
        for member in range(vises):
            slot = vises * g + member
            block = slots[slot]
            high, low = halves(cols_ref[slot])
            both = mxu(
                jnp.concatenate(halves(block), axis=0), jnp.concatenate([high, low], axis=1), NN
            )
            along = both[:tall, :BC] + both[:tall, BC:] + both[tall:, :BC]
            weight_rows = rows_ref[slot]
            model = jnp.sum(along.reshape(2, BR, BC) * weight_rows[None], axis=1)
            residual = scale_ref[slot : slot + 1, :] * (seen_ref[slot] - model)
            res_ref[slot] = residual
            out = (weight_rows[None] * residual[:, None, :]).reshape(tall, BC)
            both = mxu(
                jnp.concatenate(halves(out), axis=0), jnp.concatenate([high, low], axis=0), NT
            )
            backs.append(both[:tall, :BC] + both[:tall, BC:] + both[tall:, :BC])
        for v, sent in enumerate(exchanged(backs, ((2, 2), (1, 1)))):
            out_ref[v, at, :] = sent


def share_kernel(vises, subs, got_ref, offset_row_ref, high_ref, low_ref, out_ref):
    facet = got_ref[0]
    for f in range(1, got_ref.shape[0]):
        facet = facet + got_ref[f]
    coef = product((high_ref[...], low_ref[...]), halves(facet), NN)
    row = lax.broadcasted_iota(jnp.int32, coef.shape, 0) % (2 * RANKS)
    coef = jnp.where(row == SPARE, offset_row_ref[:1, :], coef)
    coef = coef.reshape(vises, 2 * RANKS, BC)
    for q in range(subs):
        out_ref[q * vises : (q + 1) * vises] = coef


def image_kernel(vises, subs, total, got_ref, section_ref, twist_ref, high_ref, low_ref, out_ref):
    rows = out_ref.shape[0]
    section = section_ref[...]
    first = first_pixel(rows)
    out = []
    coef = []
    for q in range(subs):
        offset = got_ref[q * vises, SPARE : SPARE + 1, :].astype(jnp.int32)
        cos_p, sin_p = angles(offset, first, total)
        cos_p, sin_p = section * cos_p, section * sin_p
        out.append(
            jnp.concatenate(
                [
                    jnp.concatenate([cos_p, -sin_p], axis=1),
                    jnp.concatenate([-sin_p, -cos_p], axis=1),
                ],
                axis=0,
            )
        )
        coef.append(jnp.concatenate([got_ref[q * vises + v] for v in range(vises)], axis=1))
    out_high, out_low = halves(jnp.concatenate(out, axis=0))
    high, low = halves(jnp.concatenate(coef, axis=0))
    grid = mxu(out_high, high, TN) + mxu(out_high, low, TN) + mxu(out_low, high, TN)
    real, imag = [], []
    for v in range(vises):
        both = stacked(grid[:, v * BC : (v + 1) * BC], (high_ref[...], low_ref[...]), NN)
        re = both[:rows, :BC] + both[rows:, BC:]
        im = both[:rows, BC:] - both[rows:, :BC]
        cos_t, sin_t = twist_ref[v : v + 1, :], twist_ref[vises + v : vises + v + 1, :]
        real.append(re * cos_t - im * sin_t)
        imag.append(re * sin_t + im * cos_t)
    even, odd = real[0] + real[2], real[1] + real[3]
    flat, turn = real[0] - real[2], imag[3] - imag[1]
    for k, part in enumerate((even + odd, flat + turn, even - odd, flat - turn)):
        out_ref[:, k * BC : (k + 1) * BC] = part


def whole():
    return pl.BlockSpec(memory_space=pltpu.VMEM)


def shards(sky, row_offsets, block_counts, block_ids, kernel_rows, kernel_cols, observed, weights):
    facets = lax.axis_size("zh") * lax.axis_size("zl")
    vises = lax.axis_size("vis")
    subs = lax.axis_size("sub")
    total = facets * K
    rows = sky.shape[0]
    lanes = K // vises
    slots = block_ids.shape[0]
    groups = slots // vises
    section, joins, grow, shares, spread, table, back_table, twist = constants(facets, vises, total)
    shares = [jnp.asarray(x) for x in shares]
    spread = jnp.asarray(spread)
    table = [jnp.asarray(x) for x in table]
    back_table = [jnp.asarray(x) for x in back_table]
    peers = NEAR * vises

    def call(kernel, name, args, outs, scratch=()):
        specs = tuple(whole() for _ in outs)
        return pl.pallas_call(
            kernel,
            out_shape=tuple(jax.ShapeDtypeStruct(x, jnp.float32) for x in outs),
            in_specs=[whole()] * len(args),
            out_specs=specs,
            scratch_shapes=list(scratch),
            compiler_params=pltpu.CompilerParams(vmem_limit_bytes=16 << 20),
            name=name,
        )(*args)

    args = (row_offsets, block_counts, block_ids, section, twist, sky, *table, weights)
    sent, scale, offset_row = pl.pallas_call(
        functools.partial(project_kernel, vises, total),
        out_shape=tuple(
            jax.ShapeDtypeStruct(x, jnp.float32)
            for x in ((peers, 16, lanes), (slots, BC), (8, lanes))
        ),
        in_specs=[pl.BlockSpec(memory_space=pltpu.HBM)] * len(args),
        out_specs=(whole(), whole(), whole()),
        scratch_shapes=[
            (pltpu.SMEM if n < 3 else pltpu.VMEM)(x.shape, x.dtype) for n, x in enumerate(args)
        ]
        + [pltpu.SemaphoreType.DMA((len(args),))],
        compiler_params=pltpu.CompilerParams(vmem_limit_bytes=123 << 19),
        name="project",
    )(*args)
    held = lax.all_to_all(sent, ("zl", "vis"), 0, 0, tiled=True)
    (sent,) = call(
        join_kernel,
        "join",
        (held, joins),
        ((facets // NEAR, GROUP_RANK // 2, lanes),),
    )
    got = lax.all_to_all(sent, "zh", 0, 0, tiled=True)

    (sent,) = call(
        functools.partial(pick_kernel, peers),
        "pick",
        (got, held, grow),
        ((peers, 2 * BR, lanes),),
        [pltpu.VMEM((peers // 8 * BC, BC), jnp.float32)],
    )
    got = lax.all_to_all(sent, ("zl", "vis"), 0, 0, tiled=True)
    exchange = (vises, groups * 2 * BR, lanes)
    residual, sent = call(
        functools.partial(degrid_kernel, vises, groups),
        "degrid",
        (got, kernel_rows, kernel_cols, observed, scale),
        ((slots, 2, BC), exchange),
    )
    got = lax.all_to_all(sent, "vis", 0, 0, tiled=True)
    (sent,) = call(
        functools.partial(place_kernel, vises, groups),
        "place",
        (got, held, spread),
        ((facets, 2 * RANK, lanes),),
    )
    got = lax.all_to_all(sent, ("zh", "zl"), 0, 0, tiled=True)

    (sent,) = call(
        functools.partial(share_kernel, vises, subs),
        "share",
        (got, offset_row, *shares),
        ((subs * vises, 2 * RANKS, lanes),),
    )
    got = lax.all_to_all(sent, ("sub", "vis"), 0, 0, tiled=True)
    (image,) = call(
        functools.partial(image_kernel, vises, subs, total),
        "image",
        (got, section, twist, *back_table),
        ((rows, K),),
    )
    return (image, residual)


def solution(mesh):
    facets, subs, vises = mesh.devices.shape
    split = mesh.devices.reshape(facets // NEAR, NEAR, subs, vises)
    return jax.shard_map(
        shards,
        mesh=jax.sharding.Mesh(split, ("zh", "zl", "sub", "vis")),
        in_specs=(
            P(("zh", "zl", "vis"), None),
            P("sub"),
            P(("zh", "zl", "sub", "vis")),
            P(("zh", "zl", "sub", "vis")),
            P(("zh", "zl", "sub", "vis"), None, None),
            P(("zh", "zl", "sub", "vis"), None, None),
            P(("zh", "zl", "sub", "vis"), None, None),
            P(("zh", "zl", "sub", "vis"), None),
        ),
        out_specs=(P(("zh", "zl", "vis"), None), P(("zh", "zl", "sub", "vis"), None, None)),
        check_vma=False,
    )
```

```python
import functools

import jax
import jax.numpy as jnp
import numpy as np
from jax import lax
from jax.experimental import pallas as pl
from jax.experimental.pallas import tpu as pltpu
from jax.sharding import PartitionSpec as P

K = 512
CR = 256
BR = 8
BC = 128
SUBS = 8
RANK = 28
NEAR = 4
GROUP_RANK = 80
RANKS = 16
SPARE = RANKS - 1


def prolate(count, band, total, rank):
    j = np.arange(count, dtype=np.float64)
    diag = -np.cos(np.pi * (2 * j - count + 1) / total) * np.cos(np.pi * band / total)
    m = np.arange(1, count, dtype=np.float64)
    off = np.sin(np.pi * m / total) * np.sin(np.pi * (count - m) / total)
    values, vectors = np.linalg.eigh(np.diag(diag) + np.diag(off, 1) + np.diag(off, -1))
    basis = vectors[:, ::-1][:, :rank]
    signs = np.sign(np.sum(basis[count // 2 :], axis=0))
    return basis * signs


def constants(facets, vises, total):
    rows = K // vises
    lanes = K // vises
    basis = prolate(K, CR, total, RANK)
    section = prolate(rows, CR, total, RANKS)
    section[:, SPARE] = 0.0
    merge = np.stack([section.T @ basis[v * rows : (v + 1) * rows] for v in range(vises)])
    r = np.arange(CR) - (CR - 1) / 2
    p = np.arange(K) - (K - 1) / 2
    kernel = np.exp(-2j * np.pi * np.outer(r, p) / total) @ basis
    centres = np.arange(facets) * K + (K - 1) / 2
    shift = np.exp(-2j * np.pi * np.outer(r, centres) / total)
    expand = shift[:, :, None] * kernel[:, None, :] * total**-0.5
    real, imag = expand.real, expand.imag
    spread = np.stack(
        [np.stack([real, -imag], axis=2), np.stack([imag, real], axis=2)], axis=0
    )
    spread = spread.reshape(2, CR // BR, BR, facets * 2 * RANK).transpose(1, 0, 2, 3)
    spread = spread.reshape(2 * CR, facets * 2 * RANK)
    merges = np.zeros((2, RANK, vises, 2, RANKS))
    for part in range(2):
        merges[part, :, :, part, :] = merge.transpose(2, 0, 1)
    merges = merges.reshape(2 * RANK, vises * 2 * RANKS)
    span = NEAR * K
    wide_basis = prolate(span, CR, total, GROUP_RANK)
    joins = np.zeros((4, GROUP_RANK, NEAR * vises, 8))
    for n in range(NEAR * vises):
        join = section.T @ wide_basis[n * rows : (n + 1) * rows]
        for j in range(4):
            joins[j, :, n] = join[8 * (j % 2) : 8 * (j % 2) + 8].T
    joins = np.stack(bf16_halves(joins.reshape(4 * GROUP_RANK, NEAR * vises * 8)))
    p = np.arange(span) - (span - 1) / 2
    kernel = np.exp(-2j * np.pi * np.outer(r, p) / total) @ wide_basis
    centres = np.arange(facets // NEAR) * span + (span - 1) / 2
    shift = np.exp(-2j * np.pi * np.outer(r, centres) / total)
    expand = shift[:, :, None] * kernel[:, None, :] * total**-0.5
    real, imag = expand.real, expand.imag
    grow = np.stack(
        [np.stack([real, -imag], axis=2), np.stack([imag, real], axis=2)], axis=0
    )
    quarter = 2 * GROUP_RANK // 4
    grow = grow.reshape(2, CR // BR, BR, facets // NEAR, 4, quarter)
    grow = grow.transpose(0, 2, 1, 4, 3, 5).reshape(2 * CR, facets // NEAR * 2 * GROUP_RANK)
    grow = np.stack(bf16_halves(grow))

    def column_table(order):
        angle = 2 * np.pi * (np.outer(np.arange(lanes), order) % lanes) / lanes
        return np.cos(angle) * K**-0.5, np.sin(angle) * K**-0.5

    index = np.arange(lanes)
    out_order = 32 * (index // 8 % 4) + 8 * (index // 32) + index % 8
    back_order = 32 * (index % 4) + index // 4
    table = bf16_halves(np.concatenate(column_table(out_order), axis=1))
    back_table = bf16_halves(np.concatenate([x.T for x in column_table(back_order)], axis=1))
    twist = 2 * np.pi * np.outer(np.arange(vises), np.arange(lanes)) / K
    twist = np.concatenate([np.cos(twist), np.sin(twist)], axis=0).astype(np.float32)
    shares = bf16_halves(merges.T)
    section = np.asarray(section.T, np.float32)
    spread = np.stack(bf16_halves(spread))
    return section, joins, grow, shares, spread, table, back_table, twist


def bf16_halves(x):
    high = x.astype(jnp.bfloat16)
    return high, (x - high.astype(np.float64)).astype(jnp.bfloat16)


def halves(x):
    high = x.astype(jnp.bfloat16)
    return high, (x - high.astype(jnp.float32)).astype(jnp.bfloat16)


def mxu(left, right, contract):
    return lax.dot_general(left, right, (contract, ((), ())), preferred_element_type=jnp.float32)


NN = ((1,), (0,))
NT = ((1,), (1,))
TN = ((0,), (0,))


def stacked(left, right, contract):
    rows = left.shape[0]
    high, low = halves(left)
    both = mxu(jnp.concatenate([high, low], axis=0), right[0], contract)
    return both[:rows] + both[rows:] + mxu(high, right[1], contract)


def product(left, right, contract):
    (lh, ll), (rh, rl) = left, right
    return mxu(lh, rh, contract) + mxu(lh, rl, contract) + mxu(ll, rh, contract)


def wide(x):
    return jnp.concatenate(halves(x), axis=1)


def angles(offset, first, total):
    pixel = first + lax.broadcasted_iota(jnp.int32, (1, BC), 1)
    turn = ((2 * offset + (CR - 1)) * pixel) % (2 * total)
    angle = turn.astype(jnp.float32) * (jnp.pi / total)
    return jnp.cos(angle), jnp.sin(angle)


def near_index():
    return lax.axis_index("zl")


def first_pixel(rows):
    facet = lax.axis_index("zh") * NEAR + near_index()
    return (facet * lax.axis_size("vis") + lax.axis_index("vis")) * rows


def exchanged(arrays, pairs):
    lane = lax.broadcasted_iota(jnp.int32, arrays[0].shape, 1)
    for step, size in pairs:
        upper = (lane // size) % 2 == 1
        after = list(arrays)
        for low in range(len(arrays)):
            if (low // step) % 2 == 0:
                one, two = arrays[low], arrays[low + step]
                after[low] = jnp.where(upper, pltpu.roll(two, size, 1), one)
                after[low + step] = jnp.where(upper, two, pltpu.roll(one, BC - size, 1))
        arrays = after
    return arrays


def project_kernel(vises, total, *refs):
    sources, rest = refs[:9], refs[9:]
    out_ref, scale_ref, offset_row_ref = rest[:3]
    targets, sem = rest[3:12], rest[12]
    copies = [
        pltpu.make_async_copy(source, target, sem.at[n])
        for n, (source, target) in enumerate(zip(sources, targets))
    ]
    for copy in copies:
        copy.start()
    for copy in copies:
        copy.wait()
    offset_ref, count_ref, id_ref, section_ref, twist_ref, sky_ref, high_ref, low_ref, wt_ref = targets
    slots = wt_ref.shape[0]
    slot = lax.broadcasted_iota(jnp.int32, wt_ref.shape, 0)
    scale_ref[...] = jnp.where(slot < count_ref[0], wt_ref[...].astype(jnp.float32), 0.0)
    lane = lax.broadcasted_iota(jnp.int32, (1, BC), 1)
    ids = jnp.zeros((1, BC), jnp.int32)
    for s in range(slots):
        ids = jnp.where((lane // 32 == s // 4) & (lane % 4 == s % 4), id_ref[s], ids)
    offset = jnp.full(offset_row_ref.shape, offset_ref[0], jnp.int32)
    offset_row_ref[...] = offset.astype(jnp.float32)
    cos_p, sin_p = angles(offset_ref[0], first_pixel(sky_ref.shape[0]), total)
    section = section_ref[...]
    into = jnp.concatenate([section * cos_p, -section * sin_p], axis=0)
    coef = stacked(into, halves(sky_ref[...]), NN)
    real, imag = [], []
    for k in range(vises):
        real.append(coef[:RANKS, k * BC : (k + 1) * BC])
        imag.append(coef[RANKS:, k * BC : (k + 1) * BC])
    re_e, re_o = real[0] + real[2], real[1] + real[3]
    im_e, im_o = imag[0] + imag[2], imag[1] + imag[3]
    re_d, re_g = real[0] - real[2], real[1] - real[3]
    im_d, im_g = imag[0] - imag[2], imag[1] - imag[3]
    folded = [
        (re_e + re_o, im_e + im_o),
        (re_d + im_g, im_d - re_g),
        (re_e - re_o, im_e - im_o),
        (re_d - im_g, im_d + re_g),
    ]
    rows = []
    for v, (re, im) in enumerate(folded):
        cos_t, sin_t = twist_ref[v : v + 1, :], twist_ref[vises + v : vises + v + 1, :]
        rows += [re * cos_t + im * sin_t, im * cos_t - re * sin_t]
    both = stacked(jnp.concatenate(rows, axis=0), (high_ref[...], low_ref[...]), NN)
    ids = jnp.broadcast_to(ids.astype(jnp.float32), (8, BC))
    chunk = lax.broadcasted_iota(jnp.int32, (8, BC), 1) // 32
    for v in range(vises):
        re = both[2 * v * RANKS : (2 * v + 1) * RANKS]
        im = both[(2 * v + 1) * RANKS : (2 * v + 2) * RANKS]
        rows = jnp.concatenate([re[:, :BC] + im[:, BC:], im[:, :BC] - re[:, BC:]], axis=0)
        for near in range(NEAR):
            packed = jnp.zeros((8, BC), jnp.float32)
            for j in range(4):
                moved = pltpu.roll(rows[8 * j : 8 * j + 8], (32 * (j - near)) % BC, 1)
                packed = jnp.where(chunk == j, moved, packed)
            out_ref[near * vises + v, :8, :] = packed
            out_ref[near * vises + v, 8:, :] = ids


def ids_columns(held_ref, vises, slots):
    row = lax.broadcasted_iota(jnp.int32, (slots, BC), 0)
    lane = lax.broadcasted_iota(jnp.int32, (slots, BC), 1)
    mine = (lane // 32 == row // 4) & (lane % 32 == row % 4)
    columns = []
    for v in range(vises):
        ids = held_ref[near_index() * vises + v, 8:, :]
        ids = jnp.concatenate([ids] * (slots // 8), axis=0)
        column = jnp.sum(jnp.where(mine, ids, 0.0), axis=1, keepdims=True)
        columns.append(jnp.broadcast_to(column, (slots, BC)).astype(jnp.int32))
    return columns


def slot_rows(columns, member, vises, groups):
    rows = []
    for v in range(vises):
        for g in range(groups):
            at = vises * g + member
            rows.append(jnp.broadcast_to(columns[v][at : at + 1], (2 * BR, BC)))
    return jnp.concatenate(rows, axis=0)


def selection(ids, bands):
    inner = lax.broadcasted_iota(jnp.int32, ids.shape, 0) % (2 * BR)
    target = (ids // bands) * (2 * BR) + inner
    lane = lax.broadcasted_iota(jnp.int32, ids.shape, 1)
    pieces = [
        jnp.where(target == lane + part * BC, 1.0, 0.0).astype(jnp.bfloat16)
        for part in range(2 * CR // BC)
    ]
    return jnp.concatenate(pieces, axis=1), ids % bands


def everywhere(x, width):
    step = BC // 2
    while step >= width:
        x = x + pltpu.roll(x, step, 1)
        step //= 2
    return x


def join_kernel(held_ref, joins_ref, out_ref):
    held = wide(held_ref[:, :8, :].reshape(joins_ref.shape[2], BC))
    rows = mxu(joins_ref[0], held, NN)
    rows = rows[:, :BC] + rows[:, BC:] + mxu(joins_ref[1], held[:, :BC], NN)
    half = GROUP_RANK // 2
    chunk = lax.broadcasted_iota(jnp.int32, (half, BC), 1) // 32
    packed = jnp.zeros((half, BC), jnp.float32)
    for part in range(2):
        at = 2 * part * GROUP_RANK
        one, two = rows[at : at + GROUP_RANK], rows[at + GROUP_RANK : at + 2 * GROUP_RANK]
        low = one[:half] + pltpu.roll(two[:half], BC - 32, 1)
        high = pltpu.roll(one[half:], 32, 1) + two[half:]
        packed = jnp.where(chunk == 2 * part, low, packed)
        packed = jnp.where(chunk == 2 * part + 1, high, packed)
    for f in range(out_ref.shape[0]):
        out_ref[f] = packed


def pick_kernel(peers, got_ref, held_ref, grow_ref, out_ref, turned_ref):
    rows = got_ref[...].reshape(got_ref.shape[0] * got_ref.shape[1], BC)
    chunk = lax.broadcasted_iota(jnp.int32, rows.shape, 1) // 32
    coef = [everywhere(jnp.where(chunk == j, rows, 0.0), 32) for j in range(4)]
    coef = wide(jnp.concatenate(coef, axis=0))
    grid = mxu(grow_ref[0], coef, NN)
    grid = grid[:, :BC] + grid[:, BC:] + mxu(grow_ref[1], coef[:, :BC], NN)
    tall, bands = 2 * BR, CR // BR
    moved = [grid] + [pltpu.roll(grid, 8 * d, 1) for d in range(1, 4)]
    eighth = lax.broadcasted_iota(jnp.int32, (bands, BC), 1) // 8
    blocks = []
    for band in range(4):
        block = jnp.zeros((bands, BC), jnp.float32)
        for zr in range(tall):
            source = moved[(zr - band) % 4][zr * bands : (zr + 1) * bands]
            block = jnp.where(eighth == zr, source, block)
        blocks.append(block)
    blocks = wide(jnp.concatenate(blocks, axis=0))
    lane = lax.broadcasted_iota(jnp.int32, (8, BC), 1)
    row = lax.broadcasted_iota(jnp.int32, (BC, BC), 0)
    hots = []
    for top in range(peers // 8):
        ids = jnp.zeros((8, BC), jnp.float32)
        for low in range(8):
            ids = jnp.where((lane // 4) % 8 == low, held_ref[8 * top + low, 8:, :], ids)
        ids = ids.astype(jnp.int32)
        target = (ids % 4) * bands + ids // 4
        target = jnp.broadcast_to(target[:1], (BC, BC))
        hots.append(jnp.where(row == target, 1.0, 0.0).astype(jnp.bfloat16))
    picked = mxu(blocks, jnp.concatenate(hots, axis=1), TN)
    picked = picked[:BC] + picked[BC:]
    for top in range(peers // 8):
        turned_ref[top * BC : (top + 1) * BC, :] = picked[:, top * BC : (top + 1) * BC]
    for top in range(peers // 8):
        parts = [turned_ref[pl.ds(top * BC + i, tall, stride=8), :] for i in range(8)]
        for low, part in enumerate(exchanged(parts, ((1, 4), (2, 8), (4, 16)))):
            out_ref[8 * top + low] = part


def place_kernel(vises, groups, part_ref, held_ref, spread_ref, out_ref):
    parts = part_ref[...].reshape(vises * groups * 2 * BR, BC)
    columns = ids_columns(held_ref, vises, vises * groups)
    piece = lax.broadcasted_iota(jnp.int32, parts.shape, 1) % vises
    turned = jnp.zeros((2 * BC, 2 * CR), jnp.float32)
    for member in range(vises):
        hot, band = selection(slot_rows(columns, member, vises, groups), K // BC)
        alone = jnp.where(piece == member, parts, 0.0)
        rows = alone
        for v in range(vises):
            if v != member:
                rows = rows + pltpu.roll(alone, (v - member) % BC, 1)
        turned = turned + mxu(wide(jnp.where(piece == band, rows, 0.0)), hot, TN)
    turned = turned[:BC] + turned[BC:]
    coef = stacked(turned, (spread_ref[0], spread_ref[1]), NN)
    out_ref[...] = coef.T.reshape(out_ref.shape)


def degrid_kernel(vises, groups, got_ref, rows_ref, cols_ref, seen_ref, scale_ref, res_ref, out_ref):
    tall = 2 * BR
    slots = [got_ref[o] for o in range(got_ref.shape[0])]
    slots = exchanged(slots, ((8, 64), (4, 32), (2, 2), (1, 1)))
    for g in range(groups):
        at = pl.ds(g * tall, tall)
        backs = []
        for member in range(vises):
            slot = vises * g + member
            block = slots[slot]
            high, low = halves(cols_ref[slot])
            both = mxu(
                jnp.concatenate(halves(block), axis=0), jnp.concatenate([high, low], axis=1), NN
            )
            along = both[:tall, :BC] + both[:tall, BC:] + both[tall:, :BC]
            weight_rows = rows_ref[slot]
            model = jnp.sum(along.reshape(2, BR, BC) * weight_rows[None], axis=1)
            residual = scale_ref[slot : slot + 1, :] * (seen_ref[slot] - model)
            res_ref[slot] = residual
            out = (weight_rows[None] * residual[:, None, :]).reshape(tall, BC)
            both = mxu(
                jnp.concatenate(halves(out), axis=0), jnp.concatenate([high, low], axis=0), NT
            )
            backs.append(both[:tall, :BC] + both[:tall, BC:] + both[tall:, :BC])
        for v, sent in enumerate(exchanged(backs, ((2, 2), (1, 1)))):
            out_ref[v, at, :] = sent


def share_kernel(vises, subs, got_ref, offset_row_ref, high_ref, low_ref, out_ref):
    facet = got_ref[0]
    for f in range(1, got_ref.shape[0]):
        facet = facet + got_ref[f]
    coef = product((high_ref[...], low_ref[...]), halves(facet), NN)
    row = lax.broadcasted_iota(jnp.int32, coef.shape, 0) % (2 * RANKS)
    coef = jnp.where(row == SPARE, offset_row_ref[:1, :], coef)
    coef = coef.reshape(vises, 2 * RANKS, BC)
    for q in range(subs):
        out_ref[q * vises : (q + 1) * vises] = coef


def image_kernel(vises, subs, total, got_ref, section_ref, twist_ref, high_ref, low_ref, out_ref):
    rows = out_ref.shape[0]
    section = section_ref[...]
    first = first_pixel(rows)
    out = []
    coef = []
    for q in range(subs):
        offset = got_ref[q * vises, SPARE : SPARE + 1, :].astype(jnp.int32)
        cos_p, sin_p = angles(offset, first, total)
        cos_p, sin_p = section * cos_p, section * sin_p
        out.append(
            jnp.concatenate(
                [
                    jnp.concatenate([cos_p, -sin_p], axis=1),
                    jnp.concatenate([-sin_p, -cos_p], axis=1),
                ],
                axis=0,
            )
        )
        coef.append(jnp.concatenate([got_ref[q * vises + v] for v in range(vises)], axis=1))
    out_high, out_low = halves(jnp.concatenate(out, axis=0))
    high, low = halves(jnp.concatenate(coef, axis=0))
    grid = mxu(out_high, high, TN) + mxu(out_high, low, TN) + mxu(out_low, high, TN)
    real, imag = [], []
    for v in range(vises):
        both = stacked(grid[:, v * BC : (v + 1) * BC], (high_ref[...], low_ref[...]), NN)
        re = both[:rows, :BC] + both[rows:, BC:]
        im = both[:rows, BC:] - both[rows:, :BC]
        cos_t, sin_t = twist_ref[v : v + 1, :], twist_ref[vises + v : vises + v + 1, :]
        real.append(re * cos_t - im * sin_t)
        imag.append(re * sin_t + im * cos_t)
    even, odd = real[0] + real[2], real[1] + real[3]
    flat, turn = real[0] - real[2], imag[3] - imag[1]
    for k, part in enumerate((even + odd, flat + turn, even - odd, flat - turn)):
        out_ref[:, k * BC : (k + 1) * BC] = part


def whole():
    return pl.BlockSpec(memory_space=pltpu.VMEM)


def shards(sky, row_offsets, block_counts, block_ids, kernel_rows, kernel_cols, observed, weights):
    facets = lax.axis_size("zh") * lax.axis_size("zl")
    vises = lax.axis_size("vis")
    subs = lax.axis_size("sub")
    total = facets * K
    rows = sky.shape[0]
    lanes = K // vises
    slots = block_ids.shape[0]
    groups = slots // vises
    section, joins, grow, shares, spread, table, back_table, twist = constants(facets, vises, total)
    shares = [jnp.asarray(x) for x in shares]
    spread = jnp.asarray(spread)
    table = [jnp.asarray(x) for x in table]
    back_table = [jnp.asarray(x) for x in back_table]
    peers = NEAR * vises

    hint = pl.CostEstimate(flops=10**10, bytes_accessed=1 << 20, transcendentals=0)

    def call(kernel, name, args, outs, scratch=()):
        specs = tuple(whole() for _ in outs)
        return pl.pallas_call(
            kernel,
            out_shape=tuple(jax.ShapeDtypeStruct(x, jnp.float32) for x in outs),
            in_specs=[whole()] * len(args),
            out_specs=specs,
            scratch_shapes=list(scratch),
            compiler_params=pltpu.CompilerParams(vmem_limit_bytes=16 << 20),
            cost_estimate=hint,
            name=name,
        )(*args)

    args = (row_offsets, block_counts, block_ids, section, twist, sky, *table, weights)
    sent, scale, offset_row = pl.pallas_call(
        functools.partial(project_kernel, vises, total),
        out_shape=tuple(
            jax.ShapeDtypeStruct(x, jnp.float32)
            for x in ((peers, 16, lanes), (slots, BC), (8, lanes))
        ),
        in_specs=[pl.BlockSpec(memory_space=pltpu.HBM)] * len(args),
        out_specs=(whole(), whole(), whole()),
        scratch_shapes=[
            (pltpu.SMEM if n < 3 else pltpu.VMEM)(x.shape, x.dtype) for n, x in enumerate(args)
        ]
        + [pltpu.SemaphoreType.DMA((len(args),))],
        compiler_params=pltpu.CompilerParams(vmem_limit_bytes=123 << 19),
        cost_estimate=hint,
        name="project",
    )(*args)
    held = lax.all_to_all(sent, ("zl", "vis"), 0, 0, tiled=True)
    (sent,) = call(
        join_kernel,
        "join",
        (held, joins),
        ((facets // NEAR, GROUP_RANK // 2, lanes),),
    )
    got = lax.all_to_all(sent, "zh", 0, 0, tiled=True)

    (sent,) = call(
        functools.partial(pick_kernel, peers),
        "pick",
        (got, held, grow),
        ((peers, 2 * BR, lanes),),
        [pltpu.VMEM((peers // 8 * BC, BC), jnp.float32)],
    )
    got = lax.all_to_all(sent, ("zl", "vis"), 0, 0, tiled=True)
    exchange = (vises, groups * 2 * BR, lanes)
    residual, sent = call(
        functools.partial(degrid_kernel, vises, groups),
        "degrid",
        (got, kernel_rows, kernel_cols, observed, scale),
        ((slots, 2, BC), exchange),
    )
    got = lax.all_to_all(sent, "vis", 0, 0, tiled=True)
    (sent,) = call(
        functools.partial(place_kernel, vises, groups),
        "place",
        (got, held, spread),
        ((facets, 2 * RANK, lanes),),
    )
    got = lax.all_to_all(sent, ("zh", "zl"), 0, 0, tiled=True)

    (sent,) = call(
        functools.partial(share_kernel, vises, subs),
        "share",
        (got, offset_row, *shares),
        ((subs * vises, 2 * RANKS, lanes),),
    )
    got = lax.all_to_all(sent, ("sub", "vis"), 0, 0, tiled=True)
    (image,) = call(
        functools.partial(image_kernel, vises, subs, total),
        "image",
        (got, section, twist, *back_table),
        ((rows, K),),
    )
    return (image, residual)


def solution(mesh):
    facets, subs, vises = mesh.devices.shape
    split = mesh.devices.reshape(facets // NEAR, NEAR, subs, vises)
    return jax.shard_map(
        shards,
        mesh=jax.sharding.Mesh(split, ("zh", "zl", "sub", "vis")),
        in_specs=(
            P(("zh", "zl", "vis"), None),
            P("sub"),
            P(("zh", "zl", "sub", "vis")),
            P(("zh", "zl", "sub", "vis")),
            P(("zh", "zl", "sub", "vis"), None, None),
            P(("zh", "zl", "sub", "vis"), None, None),
            P(("zh", "zl", "sub", "vis"), None, None),
            P(("zh", "zl", "sub", "vis"), None),
        ),
        out_specs=(P(("zh", "zl", "vis"), None), P(("zh", "zl", "sub", "vis"), None, None)),
        check_vma=False,
    )
```

```python
import functools

import jax
import jax.numpy as jnp
import numpy as np
from jax import lax
from jax.experimental import pallas as pl
from jax.experimental.pallas import tpu as pltpu
from jax.sharding import PartitionSpec as P

K = 512
CR = 256
BR = 8
BC = 128
SUBS = 8
RANK = 28
NEAR = 4
GROUP_RANK = 80
RANKS = 16
SPARE = RANKS - 1


def prolate(count, band, total, rank):
    j = np.arange(count, dtype=np.float64)
    diag = -np.cos(np.pi * (2 * j - count + 1) / total) * np.cos(np.pi * band / total)
    m = np.arange(1, count, dtype=np.float64)
    off = np.sin(np.pi * m / total) * np.sin(np.pi * (count - m) / total)
    values, vectors = np.linalg.eigh(np.diag(diag) + np.diag(off, 1) + np.diag(off, -1))
    basis = vectors[:, ::-1][:, :rank]
    signs = np.sign(np.sum(basis[count // 2 :], axis=0))
    return basis * signs


def constants(facets, vises, total):
    rows = K // vises
    lanes = K // vises
    basis = prolate(K, CR, total, RANK)
    section = prolate(rows, CR, total, RANKS)
    section[:, SPARE] = 0.0
    merge = np.stack([section.T @ basis[v * rows : (v + 1) * rows] for v in range(vises)])
    r = np.arange(CR) - (CR - 1) / 2
    p = np.arange(K) - (K - 1) / 2
    kernel = np.exp(-2j * np.pi * np.outer(r, p) / total) @ basis
    centres = np.arange(facets) * K + (K - 1) / 2
    shift = np.exp(-2j * np.pi * np.outer(r, centres) / total)
    expand = shift[:, :, None] * kernel[:, None, :] * total**-0.5
    real, imag = expand.real, expand.imag
    spread = np.stack(
        [np.stack([real, -imag], axis=2), np.stack([imag, real], axis=2)], axis=0
    )
    spread = spread.reshape(2, CR // BR, BR, facets * 2 * RANK).transpose(1, 0, 2, 3)
    spread = spread.reshape(2 * CR, facets * 2 * RANK)
    merges = np.zeros((2, RANK, vises, 2, RANKS))
    for part in range(2):
        merges[part, :, :, part, :] = merge.transpose(2, 0, 1)
    merges = merges.reshape(2 * RANK, vises * 2 * RANKS)
    span = NEAR * K
    wide_basis = prolate(span, CR, total, GROUP_RANK)
    joins = np.zeros((4, GROUP_RANK, NEAR * vises, 8))
    for n in range(NEAR * vises):
        join = section.T @ wide_basis[n * rows : (n + 1) * rows]
        for j in range(4):
            joins[j, :, n] = join[8 * (j % 2) : 8 * (j % 2) + 8].T
    joins = np.stack(bf16_halves(joins.reshape(4 * GROUP_RANK, NEAR * vises * 8)))
    p = np.arange(span) - (span - 1) / 2
    kernel = np.exp(-2j * np.pi * np.outer(r, p) / total) @ wide_basis
    centres = np.arange(facets // NEAR) * span + (span - 1) / 2
    shift = np.exp(-2j * np.pi * np.outer(r, centres) / total)
    expand = shift[:, :, None] * kernel[:, None, :] * total**-0.5
    real, imag = expand.real, expand.imag
    grow = np.stack(
        [np.stack([real, -imag], axis=2), np.stack([imag, real], axis=2)], axis=0
    )
    quarter = 2 * GROUP_RANK // 4
    grow = grow.reshape(2, CR // BR, BR, facets // NEAR, 4, quarter)
    grow = grow.transpose(0, 2, 1, 4, 3, 5).reshape(2 * CR, facets // NEAR * 2 * GROUP_RANK)
    grow = np.stack(bf16_halves(grow))

    def column_table(order):
        angle = 2 * np.pi * (np.outer(np.arange(lanes), order) % lanes) / lanes
        return np.cos(angle) * K**-0.5, np.sin(angle) * K**-0.5

    index = np.arange(lanes)
    out_order = 32 * (index // 8 % 4) + 8 * (index // 32) + index % 8
    back_order = 32 * (index % 4) + index // 4
    table = bf16_halves(np.concatenate(column_table(out_order), axis=1))
    back_table = bf16_halves(np.concatenate([x.T for x in column_table(back_order)], axis=1))
    twist = 2 * np.pi * np.outer(np.arange(vises), np.arange(lanes)) / K
    twist = np.concatenate([np.cos(twist), np.sin(twist)], axis=0).astype(np.float32)
    shares = bf16_halves(merges.T)
    section = np.asarray(section.T, np.float32)
    spread = np.stack(bf16_halves(spread))
    return section, joins, grow, shares, spread, table, back_table, twist


def bf16_halves(x):
    high = x.astype(jnp.bfloat16)
    return high, (x - high.astype(np.float64)).astype(jnp.bfloat16)


def halves(x):
    high = x.astype(jnp.bfloat16)
    return high, (x - high.astype(jnp.float32)).astype(jnp.bfloat16)


def mxu(left, right, contract):
    return lax.dot_general(left, right, (contract, ((), ())), preferred_element_type=jnp.float32)


NN = ((1,), (0,))
NT = ((1,), (1,))
TN = ((0,), (0,))


def stacked(left, right, contract):
    rows = left.shape[0]
    high, low = halves(left)
    both = mxu(jnp.concatenate([high, low], axis=0), right[0], contract)
    return both[:rows] + both[rows:] + mxu(high, right[1], contract)


def product(left, right, contract):
    (lh, ll), (rh, rl) = left, right
    return mxu(lh, rh, contract) + mxu(lh, rl, contract) + mxu(ll, rh, contract)


def wide(x):
    return jnp.concatenate(halves(x), axis=1)


def angles(offset, first, total):
    pixel = first + lax.broadcasted_iota(jnp.int32, offset.shape, 1)
    turn = ((2 * offset + (CR - 1)) * pixel) % (2 * total)
    angle = turn.astype(jnp.float32) * (jnp.pi / total)
    return jnp.cos(angle), jnp.sin(angle)


def near_index():
    return lax.axis_index("zl")


def first_pixel(rows):
    facet = lax.axis_index("zh") * NEAR + near_index()
    return (facet * lax.axis_size("vis") + lax.axis_index("vis")) * rows


def exchanged(arrays, pairs):
    lane = lax.broadcasted_iota(jnp.int32, arrays[0].shape, 1)
    for step, size in pairs:
        upper = (lane // size) % 2 == 1
        after = list(arrays)
        for low in range(len(arrays)):
            if (low // step) % 2 == 0:
                one, two = arrays[low], arrays[low + step]
                after[low] = jnp.where(upper, pltpu.roll(two, size, 1), one)
                after[low + step] = jnp.where(upper, two, pltpu.roll(one, BC - size, 1))
        arrays = after
    return arrays


def project_kernel(vises, total, *refs):
    sources, rest = refs[:9], refs[9:]
    out_ref, scale_ref, offset_row_ref = rest[:3]
    targets, sem = rest[3:12], rest[12]
    copies = [
        pltpu.make_async_copy(source, target, sem.at[n])
        for n, (source, target) in enumerate(zip(sources, targets))
    ]
    for copy in copies:
        copy.start()
    offset_ref, count_ref, id_ref, section_ref, twist_ref, sky_ref, high_ref, low_ref, wt_ref = targets
    for copy in copies[:5]:
        copy.wait()
    offset = jnp.full(offset_row_ref.shape, offset_ref[0], jnp.int32)
    offset_row_ref[...] = offset.astype(jnp.float32)
    cos_p, sin_p = angles(offset[:1], first_pixel(sky_ref.shape[0]), total)
    section = section_ref[...]
    into = jnp.concatenate([section * cos_p, -section * sin_p], axis=0)
    lane = lax.broadcasted_iota(jnp.int32, (1, BC), 1)
    ids = jnp.zeros((1, BC), jnp.int32)
    for s in range(id_ref.shape[0]):
        ids = jnp.where((lane // 32 == s // 4) & (lane % 4 == s % 4), id_ref[s], ids)
    for copy in copies[5:]:
        copy.wait()
    slot = lax.broadcasted_iota(jnp.int32, wt_ref.shape, 0)
    scale_ref[...] = jnp.where(slot < count_ref[0], wt_ref[...].astype(jnp.float32), 0.0)
    coef = stacked(into, halves(sky_ref[...]), NN)
    real, imag = [], []
    for k in range(vises):
        real.append(coef[:RANKS, k * BC : (k + 1) * BC])
        imag.append(coef[RANKS:, k * BC : (k + 1) * BC])
    re_e, re_o = real[0] + real[2], real[1] + real[3]
    im_e, im_o = imag[0] + imag[2], imag[1] + imag[3]
    re_d, re_g = real[0] - real[2], real[1] - real[3]
    im_d, im_g = imag[0] - imag[2], imag[1] - imag[3]
    folded = [
        (re_e + re_o, im_e + im_o),
        (re_d + im_g, im_d - re_g),
        (re_e - re_o, im_e - im_o),
        (re_d - im_g, im_d + re_g),
    ]
    rows = []
    for v, (re, im) in enumerate(folded):
        cos_t, sin_t = twist_ref[v : v + 1, :], twist_ref[vises + v : vises + v + 1, :]
        rows += [re * cos_t + im * sin_t, im * cos_t - re * sin_t]
    both = stacked(jnp.concatenate(rows, axis=0), (high_ref[...], low_ref[...]), NN)
    ids = jnp.broadcast_to(ids.astype(jnp.float32), (8, BC))
    chunk = lax.broadcasted_iota(jnp.int32, (8, BC), 1) // 32
    for v in range(vises):
        re = both[2 * v * RANKS : (2 * v + 1) * RANKS]
        im = both[(2 * v + 1) * RANKS : (2 * v + 2) * RANKS]
        rows = jnp.concatenate([re[:, :BC] + im[:, BC:], im[:, :BC] - re[:, BC:]], axis=0)
        for near in range(NEAR):
            packed = jnp.zeros((8, BC), jnp.float32)
            for j in range(4):
                moved = pltpu.roll(rows[8 * j : 8 * j + 8], (32 * (j - near)) % BC, 1)
                packed = jnp.where(chunk == j, moved, packed)
            out_ref[near * vises + v, :8, :] = packed
            out_ref[near * vises + v, 8:, :] = ids


def ids_columns(held_ref, vises, slots):
    row = lax.broadcasted_iota(jnp.int32, (slots, BC), 0)
    lane = lax.broadcasted_iota(jnp.int32, (slots, BC), 1)
    mine = (lane // 32 == row // 4) & (lane % 32 == row % 4)
    columns = []
    for v in range(vises):
        ids = held_ref[near_index() * vises + v, 8:, :]
        ids = jnp.concatenate([ids] * (slots // 8), axis=0)
        column = jnp.sum(jnp.where(mine, ids, 0.0), axis=1, keepdims=True)
        columns.append(jnp.broadcast_to(column, (slots, BC)).astype(jnp.int32))
    return columns


def slot_rows(columns, member, vises, groups):
    rows = []
    for v in range(vises):
        for g in range(groups):
            at = vises * g + member
            rows.append(jnp.broadcast_to(columns[v][at : at + 1], (2 * BR, BC)))
    return jnp.concatenate(rows, axis=0)


def selection(ids, bands):
    inner = lax.broadcasted_iota(jnp.int32, ids.shape, 0) % (2 * BR)
    target = (ids // bands) * (2 * BR) + inner
    lane = lax.broadcasted_iota(jnp.int32, ids.shape, 1)
    pieces = [
        jnp.where(target == lane + part * BC, 1.0, 0.0).astype(jnp.bfloat16)
        for part in range(2 * CR // BC)
    ]
    return jnp.concatenate(pieces, axis=1), ids % bands


def everywhere(x, width):
    step = BC // 2
    while step >= width:
        x = x + pltpu.roll(x, step, 1)
        step //= 2
    return x


def join_kernel(held_ref, joins_ref, out_ref):
    held = wide(held_ref[:, :8, :].reshape(joins_ref.shape[2], BC))
    rows = mxu(joins_ref[0], held, NN)
    rows = rows[:, :BC] + rows[:, BC:] + mxu(joins_ref[1], held[:, :BC], NN)
    half = GROUP_RANK // 2
    chunk = lax.broadcasted_iota(jnp.int32, (half, BC), 1) // 32
    packed = jnp.zeros((half, BC), jnp.float32)
    for part in range(2):
        at = 2 * part * GROUP_RANK
        one, two = rows[at : at + GROUP_RANK], rows[at + GROUP_RANK : at + 2 * GROUP_RANK]
        low = one[:half] + pltpu.roll(two[:half], BC - 32, 1)
        high = pltpu.roll(one[half:], 32, 1) + two[half:]
        packed = jnp.where(chunk == 2 * part, low, packed)
        packed = jnp.where(chunk == 2 * part + 1, high, packed)
    for f in range(out_ref.shape[0]):
        out_ref[f] = packed


def pick_kernel(peers, got_ref, held_ref, grow_ref, out_ref, turned_ref):
    rows = got_ref[...].reshape(got_ref.shape[0] * got_ref.shape[1], BC)
    chunk = lax.broadcasted_iota(jnp.int32, rows.shape, 1) // 32
    coef = [everywhere(jnp.where(chunk == j, rows, 0.0), 32) for j in range(4)]
    coef = wide(jnp.concatenate(coef, axis=0))
    grid = mxu(grow_ref[0], coef, NN)
    grid = grid[:, :BC] + grid[:, BC:] + mxu(grow_ref[1], coef[:, :BC], NN)
    tall, bands = 2 * BR, CR // BR
    moved = [grid] + [pltpu.roll(grid, 8 * d, 1) for d in range(1, 4)]
    eighth = lax.broadcasted_iota(jnp.int32, (bands, BC), 1) // 8
    blocks = []
    for band in range(4):
        block = jnp.zeros((bands, BC), jnp.float32)
        for zr in range(tall):
            source = moved[(zr - band) % 4][zr * bands : (zr + 1) * bands]
            block = jnp.where(eighth == zr, source, block)
        blocks.append(block)
    blocks = wide(jnp.concatenate(blocks, axis=0))
    lane = lax.broadcasted_iota(jnp.int32, (8, BC), 1)
    row = lax.broadcasted_iota(jnp.int32, (BC, BC), 0)
    hots = []
    for top in range(peers // 8):
        ids = jnp.zeros((8, BC), jnp.float32)
        for low in range(8):
            ids = jnp.where((lane // 4) % 8 == low, held_ref[8 * top + low, 8:, :], ids)
        ids = ids.astype(jnp.int32)
        target = (ids % 4) * bands + ids // 4
        target = jnp.broadcast_to(target[:1], (BC, BC))
        hots.append(jnp.where(row == target, 1.0, 0.0).astype(jnp.bfloat16))
    picked = mxu(blocks, jnp.concatenate(hots, axis=1), TN)
    picked = picked[:BC] + picked[BC:]
    for top in range(peers // 8):
        turned_ref[top * BC : (top + 1) * BC, :] = picked[:, top * BC : (top + 1) * BC]
    for top in range(peers // 8):
        parts = [turned_ref[pl.ds(top * BC + i, tall, stride=8), :] for i in range(8)]
        for low, part in enumerate(exchanged(parts, ((1, 4), (2, 8), (4, 16)))):
            out_ref[8 * top + low] = part


def place_kernel(vises, groups, part_ref, held_ref, spread_ref, out_ref):
    parts = part_ref[...].reshape(vises * groups * 2 * BR, BC)
    columns = ids_columns(held_ref, vises, vises * groups)
    piece = lax.broadcasted_iota(jnp.int32, parts.shape, 1) % vises
    turned = jnp.zeros((2 * BC, 2 * CR), jnp.float32)
    for member in range(vises):
        hot, band = selection(slot_rows(columns, member, vises, groups), K // BC)
        alone = jnp.where(piece == member, parts, 0.0)
        rows = alone
        for v in range(vises):
            if v != member:
                rows = rows + pltpu.roll(alone, (v - member) % BC, 1)
        turned = turned + mxu(wide(jnp.where(piece == band, rows, 0.0)), hot, TN)
    turned = turned[:BC] + turned[BC:]
    coef = stacked(turned, (spread_ref[0], spread_ref[1]), NN)
    out_ref[...] = coef.T.reshape(out_ref.shape)


def degrid_kernel(vises, groups, got_ref, rows_ref, cols_ref, seen_ref, scale_ref, res_ref, out_ref):
    tall = 2 * BR
    slots = [got_ref[o] for o in range(got_ref.shape[0])]
    slots = exchanged(slots, ((8, 64), (4, 32), (2, 2), (1, 1)))
    for g in range(groups):
        at = pl.ds(g * tall, tall)
        backs = []
        for member in range(vises):
            slot = vises * g + member
            block = slots[slot]
            high, low = halves(cols_ref[slot])
            both = mxu(
                jnp.concatenate(halves(block), axis=0), jnp.concatenate([high, low], axis=1), NN
            )
            along = both[:tall, :BC] + both[:tall, BC:] + both[tall:, :BC]
            weight_rows = rows_ref[slot]
            model = jnp.sum(along.reshape(2, BR, BC) * weight_rows[None], axis=1)
            residual = scale_ref[slot : slot + 1, :] * (seen_ref[slot] - model)
            res_ref[slot] = residual
            out = (weight_rows[None] * residual[:, None, :]).reshape(tall, BC)
            both = mxu(
                jnp.concatenate(halves(out), axis=0), jnp.concatenate([high, low], axis=0), NT
            )
            backs.append(both[:tall, :BC] + both[:tall, BC:] + both[tall:, :BC])
        for v, sent in enumerate(exchanged(backs, ((2, 2), (1, 1)))):
            out_ref[v, at, :] = sent


def share_kernel(vises, subs, got_ref, offset_row_ref, high_ref, low_ref, out_ref):
    facet = got_ref[0]
    for f in range(1, got_ref.shape[0]):
        facet = facet + got_ref[f]
    coef = product((high_ref[...], low_ref[...]), halves(facet), NN)
    row = lax.broadcasted_iota(jnp.int32, coef.shape, 0) % (2 * RANKS)
    coef = jnp.where(row == SPARE, offset_row_ref[:1, :], coef)
    coef = coef.reshape(vises, 2 * RANKS, BC)
    for q in range(subs):
        out_ref[q * vises : (q + 1) * vises] = coef


def image_kernel(vises, subs, total, got_ref, section_ref, twist_ref, high_ref, low_ref, out_ref):
    rows = out_ref.shape[0]
    section = section_ref[...]
    offsets = [got_ref[q * vises, SPARE : SPARE + 1, :] for q in range(subs)]
    offsets = jnp.concatenate(offsets, axis=0).astype(jnp.int32)
    cos_all, sin_all = angles(offsets, first_pixel(rows), total)
    out = []
    coef = []
    for q in range(subs):
        cos_p, sin_p = section * cos_all[q : q + 1], section * sin_all[q : q + 1]
        out.append(
            jnp.concatenate(
                [
                    jnp.concatenate([cos_p, -sin_p], axis=1),
                    jnp.concatenate([-sin_p, -cos_p], axis=1),
                ],
                axis=0,
            )
        )
        coef.append(jnp.concatenate([got_ref[q * vises + v] for v in range(vises)], axis=1))
    out = wide(jnp.concatenate(out, axis=0))
    high, low = halves(jnp.concatenate(coef, axis=0))
    grid = mxu(out, high, TN)
    grid = grid[: 2 * rows] + grid[2 * rows :] + mxu(out[:, : 2 * rows], low, TN)
    real, imag = [], []
    for v in range(vises):
        both = stacked(grid[:, v * BC : (v + 1) * BC], (high_ref[...], low_ref[...]), NN)
        re = both[:rows, :BC] + both[rows:, BC:]
        im = both[:rows, BC:] - both[rows:, :BC]
        cos_t, sin_t = twist_ref[v : v + 1, :], twist_ref[vises + v : vises + v + 1, :]
        real.append(re * cos_t - im * sin_t)
        imag.append(re * sin_t + im * cos_t)
    even, odd = real[0] + real[2], real[1] + real[3]
    flat, turn = real[0] - real[2], imag[3] - imag[1]
    for k, part in enumerate((even + odd, flat + turn, even - odd, flat - turn)):
        out_ref[:, k * BC : (k + 1) * BC] = part


def whole():
    return pl.BlockSpec(memory_space=pltpu.VMEM)


def shards(sky, row_offsets, block_counts, block_ids, kernel_rows, kernel_cols, observed, weights):
    facets = lax.axis_size("zh") * lax.axis_size("zl")
    vises = lax.axis_size("vis")
    subs = lax.axis_size("sub")
    total = facets * K
    rows = sky.shape[0]
    lanes = K // vises
    slots = block_ids.shape[0]
    groups = slots // vises
    section, joins, grow, shares, spread, table, back_table, twist = constants(facets, vises, total)
    shares = [jnp.asarray(x) for x in shares]
    spread = jnp.asarray(spread)
    table = [jnp.asarray(x) for x in table]
    back_table = [jnp.asarray(x) for x in back_table]
    peers = NEAR * vises

    hint = pl.CostEstimate(flops=10**10, bytes_accessed=1 << 20, transcendentals=0)

    def call(kernel, name, args, outs, scratch=()):
        specs = tuple(whole() for _ in outs)
        return pl.pallas_call(
            kernel,
            out_shape=tuple(jax.ShapeDtypeStruct(x, jnp.float32) for x in outs),
            in_specs=[whole()] * len(args),
            out_specs=specs,
            scratch_shapes=list(scratch),
            compiler_params=pltpu.CompilerParams(vmem_limit_bytes=16 << 20),
            cost_estimate=hint,
            name=name,
        )(*args)

    args = (row_offsets, block_counts, block_ids, section, twist, sky, *table, weights)
    sent, scale, offset_row = pl.pallas_call(
        functools.partial(project_kernel, vises, total),
        out_shape=tuple(
            jax.ShapeDtypeStruct(x, jnp.float32)
            for x in ((peers, 16, lanes), (slots, BC), (8, lanes))
        ),
        in_specs=[pl.BlockSpec(memory_space=pltpu.HBM)] * len(args),
        out_specs=(whole(), whole(), whole()),
        scratch_shapes=[
            (pltpu.SMEM if n < 3 else pltpu.VMEM)(x.shape, x.dtype) for n, x in enumerate(args)
        ]
        + [pltpu.SemaphoreType.DMA((len(args),))],
        compiler_params=pltpu.CompilerParams(vmem_limit_bytes=123 << 19),
        cost_estimate=hint,
        name="project",
    )(*args)
    held = lax.all_to_all(sent, ("zl", "vis"), 0, 0, tiled=True)
    (sent,) = call(
        join_kernel,
        "join",
        (held, joins),
        ((facets // NEAR, GROUP_RANK // 2, lanes),),
    )
    got = lax.all_to_all(sent, "zh", 0, 0, tiled=True)

    (sent,) = call(
        functools.partial(pick_kernel, peers),
        "pick",
        (got, held, grow),
        ((peers, 2 * BR, lanes),),
        [pltpu.VMEM((peers // 8 * BC, BC), jnp.float32)],
    )
    got = lax.all_to_all(sent, ("zl", "vis"), 0, 0, tiled=True)
    exchange = (vises, groups * 2 * BR, lanes)
    residual, sent = call(
        functools.partial(degrid_kernel, vises, groups),
        "degrid",
        (got, kernel_rows, kernel_cols, observed, scale),
        ((slots, 2, BC), exchange),
    )
    got = lax.all_to_all(sent, "vis", 0, 0, tiled=True)
    (sent,) = call(
        functools.partial(place_kernel, vises, groups),
        "place",
        (got, held, spread),
        ((facets, 2 * RANK, lanes),),
    )
    got = lax.all_to_all(sent, ("zh", "zl"), 0, 0, tiled=True)

    (sent,) = call(
        functools.partial(share_kernel, vises, subs),
        "share",
        (got, offset_row, *shares),
        ((subs * vises, 2 * RANKS, lanes),),
    )
    got = lax.all_to_all(sent, ("sub", "vis"), 0, 0, tiled=True)
    (image,) = call(
        functools.partial(image_kernel, vises, subs, total),
        "image",
        (got, section, twist, *back_table),
        ((rows, K),),
    )
    return (image, residual)


def solution(mesh):
    facets, subs, vises = mesh.devices.shape
    split = mesh.devices.reshape(facets // NEAR, NEAR, subs, vises)
    return jax.shard_map(
        shards,
        mesh=jax.sharding.Mesh(split, ("zh", "zl", "sub", "vis")),
        in_specs=(
            P(("zh", "zl", "vis"), None),
            P("sub"),
            P(("zh", "zl", "sub", "vis")),
            P(("zh", "zl", "sub", "vis")),
            P(("zh", "zl", "sub", "vis"), None, None),
            P(("zh", "zl", "sub", "vis"), None, None),
            P(("zh", "zl", "sub", "vis"), None, None),
            P(("zh", "zl", "sub", "vis"), None),
        ),
        out_specs=(P(("zh", "zl", "vis"), None), P(("zh", "zl", "sub", "vis"), None, None)),
        check_vma=False,
    )
```

```python
import functools

import jax
import jax.numpy as jnp
import numpy as np
from jax import lax
from jax.experimental import pallas as pl
from jax.experimental.pallas import tpu as pltpu
from jax.sharding import PartitionSpec as P

K = 512
CR = 256
BR = 8
BC = 128
SUBS = 8
RANK = 28
NEAR = 4
GROUP_RANK = 80
RANKS = 16
SPARE = RANKS - 1


def prolate(count, band, total, rank):
    j = np.arange(count, dtype=np.float64)
    diag = -np.cos(np.pi * (2 * j - count + 1) / total) * np.cos(np.pi * band / total)
    m = np.arange(1, count, dtype=np.float64)
    off = np.sin(np.pi * m / total) * np.sin(np.pi * (count - m) / total)
    values, vectors = np.linalg.eigh(np.diag(diag) + np.diag(off, 1) + np.diag(off, -1))
    basis = vectors[:, ::-1][:, :rank]
    signs = np.sign(np.sum(basis[count // 2 :], axis=0))
    return basis * signs


def constants(facets, vises, total):
    rows = K // vises
    lanes = K // vises
    basis = prolate(K, CR, total, RANK)
    section = prolate(rows, CR, total, RANKS)
    section[:, SPARE] = 0.0
    merge = np.stack([section.T @ basis[v * rows : (v + 1) * rows] for v in range(vises)])
    r = np.arange(CR) - (CR - 1) / 2
    p = np.arange(K) - (K - 1) / 2
    kernel = np.exp(-2j * np.pi * np.outer(r, p) / total) @ basis
    centres = np.arange(facets) * K + (K - 1) / 2
    shift = np.exp(-2j * np.pi * np.outer(r, centres) / total)
    expand = shift[:, :, None] * kernel[:, None, :] * total**-0.5
    real, imag = expand.real, expand.imag
    spread = np.stack(
        [np.stack([real, -imag], axis=2), np.stack([imag, real], axis=2)], axis=0
    )
    spread = spread.reshape(2, CR // BR, BR, facets * 2 * RANK).transpose(1, 0, 2, 3)
    spread = spread.reshape(2 * CR, facets * 2 * RANK)
    merges = np.zeros((2, RANK, vises, 2, RANKS))
    for part in range(2):
        merges[part, :, :, part, :] = merge.transpose(2, 0, 1)
    merges = merges.reshape(2 * RANK, vises * 2 * RANKS)
    span = NEAR * K
    wide_basis = prolate(span, CR, total, GROUP_RANK)
    joins = np.zeros((4, GROUP_RANK, NEAR * vises, 8))
    for n in range(NEAR * vises):
        join = section.T @ wide_basis[n * rows : (n + 1) * rows]
        for j in range(4):
            joins[j, :, n] = join[8 * (j % 2) : 8 * (j % 2) + 8].T
    joins = np.stack(bf16_halves(joins.reshape(4 * GROUP_RANK, NEAR * vises * 8)))
    p = np.arange(span) - (span - 1) / 2
    kernel = np.exp(-2j * np.pi * np.outer(r, p) / total) @ wide_basis
    centres = np.arange(facets // NEAR) * span + (span - 1) / 2
    shift = np.exp(-2j * np.pi * np.outer(r, centres) / total)
    expand = shift[:, :, None] * kernel[:, None, :] * total**-0.5
    real, imag = expand.real, expand.imag
    grow = np.stack(
        [np.stack([real, -imag], axis=2), np.stack([imag, real], axis=2)], axis=0
    )
    quarter = 2 * GROUP_RANK // 4
    grow = grow.reshape(2, CR // BR, BR, facets // NEAR, 4, quarter)
    grow = grow.transpose(0, 2, 1, 4, 3, 5).reshape(2 * CR, facets // NEAR * 2 * GROUP_RANK)
    grow = np.stack(bf16_halves(grow))

    def column_table(order):
        angle = 2 * np.pi * (np.outer(np.arange(lanes), order) % lanes) / lanes
        return np.cos(angle) * K**-0.5, np.sin(angle) * K**-0.5

    index = np.arange(lanes)
    out_order = 32 * (index // 8 % 4) + 8 * (index // 32) + index % 8
    back_order = 32 * (index % 4) + index // 4
    table = bf16_halves(np.concatenate(column_table(out_order), axis=1))
    back_table = bf16_halves(np.concatenate([x.T for x in column_table(back_order)], axis=1))
    twist = 2 * np.pi * np.outer(np.arange(vises), np.arange(lanes)) / K
    twist = np.concatenate([np.cos(twist), np.sin(twist)], axis=0).astype(np.float32)
    shares = bf16_halves(merges.T)
    section = np.asarray(section.T, np.float32)
    spread = np.stack(bf16_halves(spread))
    return section, joins, grow, shares, spread, table, back_table, twist


def bf16_halves(x):
    high = x.astype(jnp.bfloat16)
    return high, (x - high.astype(np.float64)).astype(jnp.bfloat16)


def halves(x):
    high = x.astype(jnp.bfloat16)
    return high, (x - high.astype(jnp.float32)).astype(jnp.bfloat16)


def mxu(left, right, contract):
    return lax.dot_general(left, right, (contract, ((), ())), preferred_element_type=jnp.float32)


NN = ((1,), (0,))
NT = ((1,), (1,))
TN = ((0,), (0,))


def stacked(left, right, contract):
    rows = left.shape[0]
    high, low = halves(left)
    both = mxu(jnp.concatenate([high, low], axis=0), right[0], contract)
    return both[:rows] + both[rows:] + mxu(high, right[1], contract)


def product(left, right, contract):
    (lh, ll), (rh, rl) = left, right
    return mxu(lh, rh, contract) + mxu(lh, rl, contract) + mxu(ll, rh, contract)


def wide(x):
    return jnp.concatenate(halves(x), axis=1)


def angles(offset, first, total):
    pixel = first + lax.broadcasted_iota(jnp.int32, offset.shape, 1)
    turn = ((2 * offset + (CR - 1)) * pixel) % (2 * total)
    angle = turn.astype(jnp.float32) * (jnp.pi / total)
    return jnp.cos(angle), jnp.sin(angle)


def near_index():
    return lax.axis_index("zl")


def first_pixel(rows):
    facet = lax.axis_index("zh") * NEAR + near_index()
    return (facet * lax.axis_size("vis") + lax.axis_index("vis")) * rows


def exchanged(arrays, pairs):
    lane = lax.broadcasted_iota(jnp.int32, arrays[0].shape, 1)
    for step, size in pairs:
        upper = (lane // size) % 2 == 1
        after = list(arrays)
        for low in range(len(arrays)):
            if (low // step) % 2 == 0:
                one, two = arrays[low], arrays[low + step]
                after[low] = jnp.where(upper, pltpu.roll(two, size, 1), one)
                after[low + step] = jnp.where(upper, two, pltpu.roll(one, BC - size, 1))
        arrays = after
    return arrays


def project_kernel(vises, total, *refs):
    sources, rest = refs[:9], refs[9:]
    out_ref, scale_ref, offset_row_ref = rest[:3]
    targets, sem = rest[3:12], rest[12]
    copies = [
        pltpu.make_async_copy(source, target, sem.at[n])
        for n, (source, target) in enumerate(zip(sources, targets))
    ]
    for copy in copies:
        copy.start()
    offset_ref, count_ref, id_ref, section_ref, twist_ref, sky_ref, high_ref, low_ref, wt_ref = targets
    for copy in copies[:5]:
        copy.wait()
    offset = jnp.full(offset_row_ref.shape, offset_ref[0], jnp.int32)
    offset_row_ref[...] = offset.astype(jnp.float32)
    cos_p, sin_p = angles(offset[:1], first_pixel(sky_ref.shape[0]), total)
    section = section_ref[...]
    into = jnp.concatenate([section * cos_p, -section * sin_p], axis=0)
    lane = lax.broadcasted_iota(jnp.int32, (1, BC), 1)
    ids = jnp.zeros((1, BC), jnp.int32)
    for s in range(id_ref.shape[0]):
        ids = jnp.where((lane // 32 == s // 4) & (lane % 4 == s % 4), id_ref[s], ids)
    for copy in copies[5:]:
        copy.wait()
    slot = lax.broadcasted_iota(jnp.int32, wt_ref.shape, 0)
    scale_ref[...] = jnp.where(slot < count_ref[0], wt_ref[...].astype(jnp.float32), 0.0)
    coef = stacked(into, halves(sky_ref[...]), NN)
    real, imag = [], []
    for k in range(vises):
        real.append(coef[:RANKS, k * BC : (k + 1) * BC])
        imag.append(coef[RANKS:, k * BC : (k + 1) * BC])
    re_e, re_o = real[0] + real[2], real[1] + real[3]
    im_e, im_o = imag[0] + imag[2], imag[1] + imag[3]
    re_d, re_g = real[0] - real[2], real[1] - real[3]
    im_d, im_g = imag[0] - imag[2], imag[1] - imag[3]
    folded = [
        (re_e + re_o, im_e + im_o),
        (re_d + im_g, im_d - re_g),
        (re_e - re_o, im_e - im_o),
        (re_d - im_g, im_d + re_g),
    ]
    rows = []
    for v, (re, im) in enumerate(folded):
        cos_t, sin_t = twist_ref[v : v + 1, :], twist_ref[vises + v : vises + v + 1, :]
        rows += [re * cos_t + im * sin_t, im * cos_t - re * sin_t]
    both = stacked(jnp.concatenate(rows, axis=0), (high_ref[...], low_ref[...]), NN)
    ids = jnp.broadcast_to(ids.astype(jnp.float32), (8, BC))
    chunk = lax.broadcasted_iota(jnp.int32, (8, BC), 1) // 32
    for v in range(vises):
        re = both[2 * v * RANKS : (2 * v + 1) * RANKS]
        im = both[(2 * v + 1) * RANKS : (2 * v + 2) * RANKS]
        rows = jnp.concatenate([re[:, :BC] + im[:, BC:], im[:, :BC] - re[:, BC:]], axis=0)
        for near in range(NEAR):
            packed = jnp.zeros((8, BC), jnp.float32)
            for j in range(4):
                moved = pltpu.roll(rows[8 * j : 8 * j + 8], (32 * (j - near)) % BC, 1)
                packed = jnp.where(chunk == j, moved, packed)
            out_ref[near * vises + v, :8, :] = packed
            out_ref[near * vises + v, 8:, :] = ids


def ids_columns(held_ref, vises, slots):
    row = lax.broadcasted_iota(jnp.int32, (slots, BC), 0)
    lane = lax.broadcasted_iota(jnp.int32, (slots, BC), 1)
    mine = (lane // 32 == row // 4) & (lane % 32 == row % 4)
    columns = []
    for v in range(vises):
        ids = held_ref[near_index() * vises + v, 8:, :]
        ids = jnp.concatenate([ids] * (slots // 8), axis=0)
        column = jnp.sum(jnp.where(mine, ids, 0.0), axis=1, keepdims=True)
        columns.append(jnp.broadcast_to(column, (slots, BC)).astype(jnp.int32))
    return columns


def slot_rows(columns, member, vises, groups):
    rows = []
    for v in range(vises):
        for g in range(groups):
            at = vises * g + member
            rows.append(jnp.broadcast_to(columns[v][at : at + 1], (2 * BR, BC)))
    return jnp.concatenate(rows, axis=0)


def selection(ids, bands):
    inner = lax.broadcasted_iota(jnp.int32, ids.shape, 0) % (2 * BR)
    target = (ids // bands) * (2 * BR) + inner
    lane = lax.broadcasted_iota(jnp.int32, ids.shape, 1)
    pieces = [
        jnp.where(target == lane + part * BC, 1.0, 0.0).astype(jnp.bfloat16)
        for part in range(2 * CR // BC)
    ]
    return jnp.concatenate(pieces, axis=1), ids % bands


def everywhere(x, width):
    step = BC // 2
    while step >= width:
        x = x + pltpu.roll(x, step, 1)
        step //= 2
    return x


def join_kernel(held_ref, joins_ref, out_ref):
    held = wide(held_ref[:, :8, :].reshape(joins_ref.shape[2], BC))
    rows = mxu(joins_ref[0], held, NN)
    rows = rows[:, :BC] + rows[:, BC:] + mxu(joins_ref[1], held[:, :BC], NN)
    half = GROUP_RANK // 2
    chunk = lax.broadcasted_iota(jnp.int32, (half, BC), 1) // 32
    packed = jnp.zeros((half, BC), jnp.float32)
    for part in range(2):
        at = 2 * part * GROUP_RANK
        one, two = rows[at : at + GROUP_RANK], rows[at + GROUP_RANK : at + 2 * GROUP_RANK]
        low = one[:half] + pltpu.roll(two[:half], BC - 32, 1)
        high = pltpu.roll(one[half:], 32, 1) + two[half:]
        packed = jnp.where(chunk == 2 * part, low, packed)
        packed = jnp.where(chunk == 2 * part + 1, high, packed)
    for f in range(out_ref.shape[0]):
        out_ref[f] = packed


def pick_kernel(peers, got_ref, held_ref, grow_ref, out_ref, turned_ref):
    rows = got_ref[...].reshape(got_ref.shape[0] * got_ref.shape[1], BC)
    chunk = lax.broadcasted_iota(jnp.int32, rows.shape, 1) // 32
    coef = [everywhere(jnp.where(chunk == j, rows, 0.0), 32) for j in range(4)]
    coef = wide(jnp.concatenate(coef, axis=0))
    grid = mxu(grow_ref[0], coef, NN)
    grid = grid[:, :BC] + grid[:, BC:] + mxu(grow_ref[1], coef[:, :BC], NN)
    tall, bands = 2 * BR, CR // BR
    moved = [grid] + [pltpu.roll(grid, 8 * d, 1) for d in range(1, 4)]
    eighth = lax.broadcasted_iota(jnp.int32, (bands, BC), 1) // 8
    blocks = []
    for band in range(4):
        block = jnp.zeros((bands, BC), jnp.float32)
        for zr in range(tall):
            source = moved[(zr - band) % 4][zr * bands : (zr + 1) * bands]
            block = jnp.where(eighth == zr, source, block)
        blocks.append(block)
    blocks = wide(jnp.concatenate(blocks, axis=0))
    lane = lax.broadcasted_iota(jnp.int32, (8, BC), 1)
    row = lax.broadcasted_iota(jnp.int32, (BC, BC), 0)
    hots = []
    for top in range(peers // 8):
        ids = jnp.zeros((8, BC), jnp.float32)
        for low in range(8):
            ids = jnp.where((lane // 4) % 8 == low, held_ref[8 * top + low, 8:, :], ids)
        ids = ids.astype(jnp.int32)
        target = (ids % 4) * bands + ids // 4
        target = jnp.broadcast_to(target[:1], (BC, BC))
        hots.append(jnp.where(row == target, 1.0, 0.0).astype(jnp.bfloat16))
    picked = mxu(blocks, jnp.concatenate(hots, axis=1), TN)
    picked = picked[:BC] + picked[BC:]
    for top in range(peers // 8):
        turned_ref[top * BC : (top + 1) * BC, :] = picked[:, top * BC : (top + 1) * BC]
    for top in range(peers // 8):
        parts = [turned_ref[pl.ds(top * BC + i, tall, stride=8), :] for i in range(8)]
        for low, part in enumerate(exchanged(parts, ((1, 4), (2, 8), (4, 16)))):
            out_ref[8 * top + low] = part


def place_kernel(vises, groups, part_ref, held_ref, spread_ref, out_ref):
    parts = part_ref[...].reshape(vises * groups * 2 * BR, BC)
    columns = ids_columns(held_ref, vises, vises * groups)
    piece = lax.broadcasted_iota(jnp.int32, parts.shape, 1) % vises
    left, right = [], []
    for member in range(vises):
        hot, band = selection(slot_rows(columns, member, vises, groups), K // BC)
        alone = jnp.where(piece == member, parts, 0.0)
        rows = alone
        for v in range(vises):
            if v != member:
                rows = rows + pltpu.roll(alone, (v - member) % BC, 1)
        left.append(wide(jnp.where(piece == band, rows, 0.0)))
        right.append(hot)
    turned = mxu(jnp.concatenate(left, axis=0), jnp.concatenate(right, axis=0), TN)
    turned = turned[:BC] + turned[BC:]
    coef = stacked(turned, (spread_ref[0], spread_ref[1]), NN)
    out_ref[...] = coef.T.reshape(out_ref.shape)


def degrid_kernel(vises, groups, got_ref, rows_ref, cols_ref, seen_ref, scale_ref, res_ref, out_ref):
    tall = 2 * BR
    slots = [got_ref[o] for o in range(got_ref.shape[0])]
    slots = exchanged(slots, ((8, 64), (4, 32), (2, 2), (1, 1)))
    for g in range(groups):
        at = pl.ds(g * tall, tall)
        backs = []
        for member in range(vises):
            slot = vises * g + member
            block = slots[slot]
            high, low = halves(cols_ref[slot])
            both = mxu(
                jnp.concatenate(halves(block), axis=0), jnp.concatenate([high, low], axis=1), NN
            )
            along = both[:tall, :BC] + both[:tall, BC:] + both[tall:, :BC]
            weight_rows = rows_ref[slot]
            model = jnp.sum(along.reshape(2, BR, BC) * weight_rows[None], axis=1)
            residual = scale_ref[slot : slot + 1, :] * (seen_ref[slot] - model)
            res_ref[slot] = residual
            out = (weight_rows[None] * residual[:, None, :]).reshape(tall, BC)
            both = mxu(
                jnp.concatenate(halves(out), axis=0), jnp.concatenate([high, low], axis=0), NT
            )
            backs.append(both[:tall, :BC] + both[:tall, BC:] + both[tall:, :BC])
        for v, sent in enumerate(exchanged(backs, ((2, 2), (1, 1)))):
            out_ref[v, at, :] = sent


def share_kernel(vises, subs, got_ref, offset_row_ref, high_ref, low_ref, out_ref):
    facet = got_ref[0]
    for f in range(1, got_ref.shape[0]):
        facet = facet + got_ref[f]
    coef = product((high_ref[...], low_ref[...]), halves(facet), NN)
    row = lax.broadcasted_iota(jnp.int32, coef.shape, 0) % (2 * RANKS)
    coef = jnp.where(row == SPARE, offset_row_ref[:1, :], coef)
    coef = coef.reshape(vises, 2 * RANKS, BC)
    for q in range(subs):
        out_ref[q * vises : (q + 1) * vises] = coef


def image_kernel(vises, subs, total, got_ref, section_ref, twist_ref, high_ref, low_ref, out_ref):
    rows = out_ref.shape[0]
    section = section_ref[...]
    offsets = [got_ref[q * vises, SPARE : SPARE + 1, :] for q in range(subs)]
    offsets = jnp.concatenate(offsets, axis=0).astype(jnp.int32)
    cos_all, sin_all = angles(offsets, first_pixel(rows), total)
    out = []
    coef = []
    for q in range(subs):
        cos_p, sin_p = section * cos_all[q : q + 1], section * sin_all[q : q + 1]
        out.append(
            jnp.concatenate(
                [
                    jnp.concatenate([cos_p, -sin_p], axis=1),
                    jnp.concatenate([-sin_p, -cos_p], axis=1),
                ],
                axis=0,
            )
        )
        coef.append(jnp.concatenate([got_ref[q * vises + v] for v in range(vises)], axis=1))
    out = wide(jnp.concatenate(out, axis=0))
    high, low = halves(jnp.concatenate(coef, axis=0))
    grid = mxu(out, high, TN)
    grid = grid[: 2 * rows] + grid[2 * rows :] + mxu(out[:, : 2 * rows], low, TN)
    real, imag = [], []
    for v in range(vises):
        both = stacked(grid[:, v * BC : (v + 1) * BC], (high_ref[...], low_ref[...]), NN)
        re = both[:rows, :BC] + both[rows:, BC:]
        im = both[:rows, BC:] - both[rows:, :BC]
        cos_t, sin_t = twist_ref[v : v + 1, :], twist_ref[vises + v : vises + v + 1, :]
        real.append(re * cos_t - im * sin_t)
        imag.append(re * sin_t + im * cos_t)
    even, odd = real[0] + real[2], real[1] + real[3]
    flat, turn = real[0] - real[2], imag[3] - imag[1]
    for k, part in enumerate((even + odd, flat + turn, even - odd, flat - turn)):
        out_ref[:, k * BC : (k + 1) * BC] = part


def whole():
    return pl.BlockSpec(memory_space=pltpu.VMEM)


def shards(sky, row_offsets, block_counts, block_ids, kernel_rows, kernel_cols, observed, weights):
    facets = lax.axis_size("zh") * lax.axis_size("zl")
    vises = lax.axis_size("vis")
    subs = lax.axis_size("sub")
    total = facets * K
    rows = sky.shape[0]
    lanes = K // vises
    slots = block_ids.shape[0]
    groups = slots // vises
    section, joins, grow, shares, spread, table, back_table, twist = constants(facets, vises, total)
    shares = [jnp.asarray(x) for x in shares]
    spread = jnp.asarray(spread)
    table = [jnp.asarray(x) for x in table]
    back_table = [jnp.asarray(x) for x in back_table]
    peers = NEAR * vises

    hint = pl.CostEstimate(flops=10**10, bytes_accessed=1 << 20, transcendentals=0)

    def call(kernel, name, args, outs, scratch=()):
        specs = tuple(whole() for _ in outs)
        return pl.pallas_call(
            kernel,
            out_shape=tuple(jax.ShapeDtypeStruct(x, jnp.float32) for x in outs),
            in_specs=[whole()] * len(args),
            out_specs=specs,
            scratch_shapes=list(scratch),
            compiler_params=pltpu.CompilerParams(vmem_limit_bytes=16 << 20),
            cost_estimate=hint,
            name=name,
        )(*args)

    args = (row_offsets, block_counts, block_ids, section, twist, sky, *table, weights)
    sent, scale, offset_row = pl.pallas_call(
        functools.partial(project_kernel, vises, total),
        out_shape=tuple(
            jax.ShapeDtypeStruct(x, jnp.float32)
            for x in ((peers, 16, lanes), (slots, BC), (8, lanes))
        ),
        in_specs=[pl.BlockSpec(memory_space=pltpu.HBM)] * len(args),
        out_specs=(whole(), whole(), whole()),
        scratch_shapes=[
            (pltpu.SMEM if n < 3 else pltpu.VMEM)(x.shape, x.dtype) for n, x in enumerate(args)
        ]
        + [pltpu.SemaphoreType.DMA((len(args),))],
        compiler_params=pltpu.CompilerParams(vmem_limit_bytes=123 << 19),
        cost_estimate=hint,
        name="project",
    )(*args)
    held = lax.all_to_all(sent, ("zl", "vis"), 0, 0, tiled=True)
    (sent,) = call(
        join_kernel,
        "join",
        (held, joins),
        ((facets // NEAR, GROUP_RANK // 2, lanes),),
    )
    got = lax.all_to_all(sent, "zh", 0, 0, tiled=True)

    (sent,) = call(
        functools.partial(pick_kernel, peers),
        "pick",
        (got, held, grow),
        ((peers, 2 * BR, lanes),),
        [pltpu.VMEM((peers // 8 * BC, BC), jnp.float32)],
    )
    got = lax.all_to_all(sent, ("zl", "vis"), 0, 0, tiled=True)
    exchange = (vises, groups * 2 * BR, lanes)
    residual, sent = call(
        functools.partial(degrid_kernel, vises, groups),
        "degrid",
        (got, kernel_rows, kernel_cols, observed, scale),
        ((slots, 2, BC), exchange),
    )
    got = lax.all_to_all(sent, "vis", 0, 0, tiled=True)
    (sent,) = call(
        functools.partial(place_kernel, vises, groups),
        "place",
        (got, held, spread),
        ((facets, 2 * RANK, lanes),),
    )
    got = lax.all_to_all(sent, ("zh", "zl"), 0, 0, tiled=True)

    (sent,) = call(
        functools.partial(share_kernel, vises, subs),
        "share",
        (got, offset_row, *shares),
        ((subs * vises, 2 * RANKS, lanes),),
    )
    got = lax.all_to_all(sent, ("sub", "vis"), 0, 0, tiled=True)
    (image,) = call(
        functools.partial(image_kernel, vises, subs, total),
        "image",
        (got, section, twist, *back_table),
        ((rows, K),),
    )
    return (image, residual)


def solution(mesh):
    facets, subs, vises = mesh.devices.shape
    split = mesh.devices.reshape(facets // NEAR, NEAR, subs, vises)
    return jax.shard_map(
        shards,
        mesh=jax.sharding.Mesh(split, ("zh", "zl", "sub", "vis")),
        in_specs=(
            P(("zh", "zl", "vis"), None),
            P("sub"),
            P(("zh", "zl", "sub", "vis")),
            P(("zh", "zl", "sub", "vis")),
            P(("zh", "zl", "sub", "vis"), None, None),
            P(("zh", "zl", "sub", "vis"), None, None),
            P(("zh", "zl", "sub", "vis"), None, None),
            P(("zh", "zl", "sub", "vis"), None),
        ),
        out_specs=(P(("zh", "zl", "vis"), None), P(("zh", "zl", "sub", "vis"), None, None)),
        check_vma=False,
    )
```
